32 devices in a mesh: groups: 2 (over x), img: 16 (over z, y, core).
Axes of the slice: x: 2, y: 2, z: 4, core: 2. Of those that a mesh axis runs over, the one named last changes fastest.
Arguments:
- images: bfloat16 [256, 4608], P(('groups', 'img')), parts along dimension 0, may hold values from -64 to 64
- class_refs: bfloat16 [96, 4608], P('groups', 'img'), parts along dimension 0, may hold values from -0.6 to 0.6
- sigma2: float32 [32, 16], P('groups'), parts along dimension 0, may hold values from 0.5 to 18
- ctf_group: int32 [256], P(('groups', 'img')), parts along dimension 0, may hold values from 0 to 15, as said below
- defocus_bin: int32 [256], P(('groups', 'img')), parts along dimension 0, may hold values from 0 to 31
Outputs:
- new_refs: float32 [96, 4608], P('groups', 'img'), parts along dimension 0
The draws below stay inside these ranges and needn't reach their ends.
There are 2 independent parts, one for each index of `groups`. The reference program is written for one: setup_inputs(seed, part) draws one part's arguments, and reference() takes and returns one part's arrays. A program takes and returns all parts, laid end to end along the dimension named above; each array names one. Nothing has to cross between parts.
Inputs may be any that keep to these rules, and one draw needn't show every extreme that they name: `ctf_group`: never falls from one image to the next; every group appears.
All inputs are finite; a program needn't handle non-finite values.
Results may differ from the reference program's by a relative error of at most 0.0084.
Values may be sent and summed in bfloat16 or wider, within the bound.
A program may use at most 128 MiB of HBM per device.

```python
import math
import jax
import jax.numpy as jnp
from jax import lax

CLASSES = 48
ROT = 36
SHELLS = 16
ANG = 144
REACH = 3
SHIFTS = 49
BINS = 32
NGROUP = 16
IMAGES = 128


def group_ids(key):
    extra = jax.random.randint(jax.random.fold_in(key, 11), (IMAGES - NGROUP,), 0, NGROUP)
    joined = jnp.concatenate([jnp.arange(NGROUP, dtype=jnp.int32), extra.astype(jnp.int32)])
    return jnp.sort(joined)


def bin_ids(key):
    return jax.random.randint(jax.random.fold_in(key, 13), (IMAGES,), 0, BINS).astype(jnp.int32)


def noise_table(key, rise):
    level = jnp.arange(NGROUP, dtype=jnp.float32) / max(NGROUP - 1, 1)
    base = jnp.exp(jax.random.uniform(jax.random.fold_in(key, 17), (NGROUP, SHELLS), jnp.float32, math.log(0.5), math.log(2.0)))
    return base * rise ** level[:, None]


def reference_table(key):
    values = jax.random.normal(jax.random.fold_in(key, 21), (CLASSES, 2, SHELLS, ANG), jnp.float32)
    return 0.1 * jnp.clip(values, -6.0, 6.0)


def draw_ctf_group(key, part):
    return group_ids(key)


def draw_defocus_bin(key, part):
    return bin_ids(key)


def draw_sigma2(key, part):
    return noise_table(key, 3.0)


def draw_class_refs(key, part):
    table = reference_table(key)
    return table.reshape(CLASSES, 2 * SHELLS * ANG).astype(jnp.bfloat16)


def draw_images(key, part):
    values = jax.random.normal(jax.random.fold_in(key, 31), (IMAGES, 2 * SHELLS * ANG), jnp.float32)
    return jnp.clip(values, -6.0, 6.0).astype(jnp.bfloat16)


def setup_inputs(seed: int = 0, part: int = 0) -> dict:
    keys = jax.random.split(jax.random.key(seed), 6)
    part_keys = jax.random.split(jax.random.fold_in(keys[5], part), 6)
    images = draw_images(jax.random.fold_in(jax.random.fold_in(keys[5], part), 71), part)
    class_refs = draw_class_refs(jax.random.fold_in(jax.random.fold_in(keys[5], part), 71), part)
    sigma2 = draw_sigma2(jax.random.fold_in(jax.random.fold_in(keys[5], part), 71), part)
    ctf_group = draw_ctf_group(jax.random.fold_in(jax.random.fold_in(keys[5], part), 71), part)
    defocus_bin = draw_defocus_bin(jax.random.fold_in(jax.random.fold_in(keys[5], part), 71), part)
    return dict(images=images, class_refs=class_refs, sigma2=sigma2, ctf_group=ctf_group, defocus_bin=defocus_bin)


def shell_radius():
    return (jnp.arange(SHELLS, dtype=jnp.float32) + 1.0) / (2.0 * SHELLS)


def ctf_table():
    defocus = 1.0 + jnp.arange(BINS, dtype=jnp.float32) / BINS
    radius = shell_radius()
    return -jnp.sin(80.0 * defocus[:, None] * radius[None, :] ** 2 + 0.1)


def phase_tables():
    offsets = jnp.arange(2 * REACH + 1, dtype=jnp.float32) - REACH
    shift_x = jnp.repeat(offsets, 2 * REACH + 1)
    shift_y = jnp.tile(offsets, 2 * REACH + 1)
    angles = 2.0 * math.pi * jnp.arange(ANG, dtype=jnp.float32) / ANG
    radius = shell_radius()
    phase = 2.0 * math.pi * radius[None, :, None] * (
        jnp.cos(angles)[None, None, :] * shift_x[:, None, None]
        + jnp.sin(angles)[None, None, :] * shift_y[:, None, None])
    return jnp.cos(phase), jnp.sin(phase)


def image_weights(ctf_group, defocus_bin, sigma2):
    bin_hot = (defocus_bin[:, None] == jnp.arange(BINS, dtype=jnp.int32)[None, :]).astype(jnp.float32)
    group_hot = (ctf_group[:, None] == jnp.arange(NGROUP, dtype=jnp.int32)[None, :]).astype(jnp.float32)
    ctf_sel = jnp.dot(bin_hot, ctf_table(), precision=lax.Precision.HIGHEST)
    noise_sel = jnp.dot(group_hot, sigma2, precision=lax.Precision.HIGHEST)
    return ctf_sel / noise_sel, ctf_sel * ctf_sel / noise_sel


def shifted_features(images, filter_weight):
    count_img = images.shape[0]
    pixels = images.astype(jnp.float32).reshape(count_img, 2, SHELLS, ANG)
    real_part = pixels[:, 0] * filter_weight[:, :, None]
    imag_part = pixels[:, 1] * filter_weight[:, :, None]
    cosine, sine_table = phase_tables()
    shifted_real = real_part[:, None] * cosine[None] - imag_part[:, None] * sine_table[None]
    shifted_imag = real_part[:, None] * sine_table[None] + imag_part[:, None] * cosine[None]
    stacked = jnp.stack([shifted_real, shifted_imag], axis=2)
    return stacked.reshape(count_img * SHIFTS, 2 * SHELLS * ANG).astype(jnp.bfloat16)


def reference(images, class_refs, sigma2, ctf_group, defocus_bin):
    count_img = images.shape[0]
    angle_step = ANG // ROT
    filter_weight, shell_weight = image_weights(ctf_group, defocus_bin, sigma2)
    features = shifted_features(images, filter_weight)
    refs_four = class_refs.reshape(CLASSES, 2, SHELLS, ANG)
    rotated = jnp.concatenate([jnp.roll(refs_four, turn_index * angle_step, axis=3) for turn_index in range(ROT)], axis=0)
    rotated = rotated.reshape(ROT * CLASSES, 2 * SHELLS * ANG)
    cross = jnp.dot(features, rotated.T, preferred_element_type=jnp.float32)
    shell_power = jnp.sum(jnp.square(refs_four.astype(jnp.float32)), axis=(1, 3))
    quadratic = 0.5 * jnp.dot(shell_weight, shell_power.T, precision=lax.Precision.HIGHEST)
    scores = cross.reshape(count_img, SHIFTS, ROT, CLASSES) - quadratic[:, None, None, :]
    highest = jnp.max(scores, axis=(1, 2, 3), keepdims=True)
    expanded = jnp.exp(scores - highest)
    normalizer = jnp.sum(expanded, axis=(1, 2, 3), keepdims=True)
    posterior = expanded / normalizer
    occupancy = jnp.sum(posterior, axis=(1, 2))
    posterior_b = posterior.astype(jnp.bfloat16).reshape(count_img * SHIFTS, ROT * CLASSES)
    oriented = jnp.dot(posterior_b.T, features, preferred_element_type=jnp.float32)
    oriented = oriented.reshape(ROT, CLASSES, 2, SHELLS, ANG)
    numerator = jnp.zeros((CLASSES, 2, SHELLS, ANG), jnp.float32)
    for turn_index in range(ROT):
        numerator = numerator + jnp.roll(oriented[turn_index], -turn_index * angle_step, axis=3)
    weights = jnp.dot(occupancy.T, shell_weight, precision=lax.Precision.HIGHEST)
    new_refs = numerator / (weights[:, None, :, None] + 1.0)
    return new_refs.reshape(CLASSES, 2 * SHELLS * ANG)
```

```python
import math

import jax
import jax.numpy as jnp
import numpy as np
from jax import lax
from jax.experimental import pallas as pl
from jax.experimental.pallas import tpu as pltpu
from jax.sharding import PartitionSpec as P

CLASSES = 48
ROT = 36
SHELLS = 16
ANG = 144
REACH = 3
SHIFTS = 49
BINS = 32
NGROUP = 16

LANES = 128
PARTS = 2 * SHELLS
STEP = ANG // ROT
SPAN = STEP * PARTS
WIDTH = ROT * SPAN
SIDE = 2 * REACH + 1
PAIRS = ROT // 2
TILES = (SHIFTS + 1) // 2
SLOTS = SIDE + 2
BIG = 1e30
EXACT = lax.Precision.HIGHEST


def phase_parts():
    angles = 2.0 * np.pi * np.arange(ANG) / ANG
    radius = (np.arange(SHELLS) + 1.0) / (2.0 * SHELLS)
    tables = []
    for direction in (np.sin(angles), np.cos(angles)):
        for offset in range(1, REACH + 1):
            phase = 2.0 * np.pi * offset * direction[None, :] * radius[:, None]
            both = []
            for cosine, sine in ((np.cos(phase), -np.sin(phase)), (np.cos(phase), np.sin(phase))):
                both.append(np.stack([cosine, sine]))
            table = np.stack(both, axis=1)
            table = table.reshape(2, PARTS, ROT, STEP).transpose(0, 2, 1, 3)
            tables.append(table.reshape(2, ROT, SPAN))
    tables.append(np.ones((2, ROT, SPAN)))
    return np.stack(tables).astype(np.float32)


def ctf_lanes():
    radius = (np.arange(SHELLS) + 1.0) / (2.0 * SHELLS)
    defocus = 1.0 + np.arange(BINS) / BINS
    table = -np.sin(80.0 * defocus[:, None] * radius**2 + 0.1)
    return np.tile(np.repeat(table, STEP, axis=1), (1, 2)).astype(np.float32)


def channel_order():
    table = np.zeros((SPAN, SPAN), np.float32)
    for t in range(STEP):
        for p in range(PARTS):
            table[t * PARTS + p, p * STEP + t] = 1.0
    return table


COS9 = [math.cos(2.0 * math.pi * k / 9.0) for k in range(5)]
SIN9 = [math.sin(2.0 * math.pi * k / 9.0) for k in range(5)]


def even9(first, s1, s2, s3, s4):
    c1, c2 = COS9[1], COS9[2]
    a, b = s1 - s4, s2 - s4
    g1 = c1 * a + c2 * b
    g2 = c2 * (a - b) - c1 * b
    t = s1 + s2 + s4
    w = first + s3
    u = first - 0.5 * s3
    return [w + t, u + g1, u + g2, w - 0.5 * t, u - (g1 + g2)]


def odd9(d1, d2, d3, d4):
    n1, n3, n4 = SIN9[1], SIN9[3], SIN9[4]
    a, b, c = d1 + d2, d2 + d4, d1 - d4
    h1 = n1 * a + n4 * b
    h2 = n1 * c + n4 * a
    e = n3 * d3
    return [h1 + e, h2 - e, n3 * (d1 - d2 + d4), h2 - h1 + e]


def where_q(a, b):
    return (9 * a + 4 * b) % ROT


def dft36(load):
    parts = []
    for a in range(4):
        x = [load(where_q(a, b)) for b in range(9)]
        s = [x[j] + x[9 - j] for j in range(1, 5)]
        d = [x[9 - j] - x[j] for j in range(1, 5)]
        parts.append((even9(x[0], *s), [None] + odd9(*d)))
    y = [part[0][0] for part in parts]
    p, m = y[0] + y[2], y[1] + y[3]
    pairs = [(p + m, p - m), (y[0] - y[2], y[3] - y[1])]
    for g in range(1, 5):
        re = [part[0][g] for part in parts]
        im = [part[1][g] for part in parts]
        rp, rm, ip, im_ = re[0] + re[2], re[0] - re[2], im[0] + im[2], im[0] - im[2]
        sp, sm, jp, jm = re[1] + re[3], re[1] - re[3], im[1] + im[3], im[1] - im[3]
        pairs.append((rp + sp, ip + jp))
        pairs.append((rm + jm, im_ - sm))
        pairs.append((rp - sp, ip - jp))
        pairs.append((rm - jm, im_ + sm))
    return pairs


def idft36(pairs):
    p, m = pairs[0][0] + pairs[0][1], pairs[0][0] - pairs[0][1]
    re, im = pairs[1]
    parts = [[(p + re, None)], [(m - im, None)], [(p - re, None)], [(m + im, None)]]
    for g in range(4):
        (r0, i0), (r1, i1), (r2, i2), (r3, i3) = pairs[2 + 4 * g : 6 + 4 * g]
        rp, rm, ip, im_ = r0 + r2, r0 - r2, i0 + i2, i0 - i2
        sp, sm, jp, jm = r1 + r3, r1 - r3, i1 + i3, i1 - i3
        parts[0].append((rp + sp, ip + jp))
        parts[1].append((rm - jm, im_ + sm))
        parts[2].append((rp - sp, ip - jp))
        parts[3].append((rm + jm, im_ - sm))
    out = [None] * ROT
    for a in range(4):
        y = parts[a]
        even = even9(y[0][0], y[1][0], y[2][0], y[3][0], y[4][0])
        odd = [None] + odd9(y[1][1], y[2][1], y[3][1], y[4][1])
        out[where_q(a, 0)] = even[0]
        for b in range(1, 5):
            out[where_q(a, b)] = even[b] - odd[b]
            out[where_q(a, 9 - b)] = even[b] + odd[b]
    return out


def split(value):
    high = value.astype(jnp.bfloat16)
    return high, (value - high.astype(jnp.float32)).astype(jnp.bfloat16)


def geometry(share):
    piece = min(share, ANG)
    halves = ANG // piece
    pieces = share // piece
    turns = piece // STEP
    width = turns * CLASSES
    padded = -(-(width + CLASSES) // LANES) * LANES
    return piece, halves, pieces, turns, width, padded


def em_kernel(
    count_dev,
    img_ref,
    refs_ref,
    sigma_ref,
    group_ref,
    bin_ref,
    ctf_ref,
    phase_ref,
    perm_ref,
    out_ref,
    turned_img,
    moved,
    fhi,
    flo,
    rhat,
    xs,
    numh,
    flat,
    cols_t,
    fin,
    mine,
    got,
    pay,
    mid,
    mixed,
    final,
    near_send,
    near_recv,
    far_send,
    far_recv,
    pair_send,
    pair_recv,
    last_send,
    last_recv,
):
    rows = CLASSES
    count_img = img_ref.shape[0]
    share = refs_ref.shape[1]
    piece, halves, pieces, turns, width, padded = geometry(share)
    group_rows = STEP * pieces
    count_n = fhi.shape[1]
    half = count_dev // 2
    me = lax.axis_index("img")
    core = lax.rem(me, 2)
    place = lax.div(me, 2)
    partner = me + 1 - 2 * core
    f32, bf16 = jnp.float32, jnp.bfloat16

    def ahead(offset):
        return lax.rem(place + offset, half)

    def behind(offset):
        return lax.rem(place + half - offset, half)

    barrier = pltpu.get_barrier_semaphore()
    for offset in range(1, half):
        pl.semaphore_signal(
            barrier,
            inc=1,
            device_id={"img": 2 * ahead(offset) + core},
            device_id_type=pl.DeviceIdType.MESH,
        )
    pl.semaphore_signal(
        barrier, inc=1, device_id={"img": partner}, device_id_type=pl.DeviceIdType.MESH
    )

    def remote(source, target, send, recv, device):
        return pltpu.make_async_remote_copy(
            src_ref=source,
            dst_ref=target,
            send_sem=send,
            recv_sem=recv,
            device_id={"img": device},
            device_id_type=pl.DeviceIdType.MESH,
        )

    fin[...] = refs_ref[...].astype(f32).T
    turned = []
    for q in range(turns):
        turned.append(
            jnp.concatenate(
                [fin[i * piece + q * STEP : i * piece + (q + 1) * STEP, :] for i in range(pieces)],
                axis=0,
            )
        )
    turned.append(jnp.zeros((group_rows, padded - width), f32))
    own = jnp.concatenate(turned, axis=1).astype(bf16)
    mine[...] = own
    got[me] = own
    pl.semaphore_wait(barrier, half)

    far = [
        remote(
            mine,
            got.at[me],
            far_send.at[offset],
            far_recv.at[offset],
            2 * ahead(offset) + core,
        )
        for offset in range(1, half)
    ]
    near = [remote(mine, got.at[me], near_send.at[0], near_recv.at[0], partner)]
    for copy in far + near:
        copy.start()

    for part in range(PARTS):
        block = img_ref[:, part * ANG : (part + 1) * ANG].astype(f32)
        turned_img[pl.ds(part, ANG, stride=PARTS), :] = block.T

    def pick(ids, table):
        hot = ids == lax.broadcasted_iota(jnp.int32, (table.shape[0], count_img), 0)
        return lax.dot_general(
            hot.astype(f32),
            table,
            (((0,), (0,)), ((), ())),
            precision=EXACT,
            preferred_element_type=f32,
        )

    lane_shell = lax.rem(
        lax.div(lax.broadcasted_iota(jnp.int32, (SHELLS, SPAN), 1), STEP), SHELLS
    )
    spread = (lane_shell == lax.broadcasted_iota(jnp.int32, (SHELLS, SPAN), 0)).astype(f32)
    noise = jnp.dot(
        pick(group_ref[...], sigma_ref[...]), spread, precision=EXACT, preferred_element_type=f32
    )
    ctf = pick(bin_ref[...], ctf_ref[...])
    weight = ctf / noise
    shell_w = jnp.concatenate([ctf * ctf / noise] * (LANES // count_img), axis=0)

    base = jnp.concatenate(
        [turned_img[q * SPAN : (q + 1) * SPAN, :].T for q in range(ROT)], axis=0
    ).astype(bf16)
    base = jnp.dot(base, perm_ref[...], preferred_element_type=f32)
    for q in range(ROT):
        at = slice(q * count_img, (q + 1) * count_img)
        value = base[at] * weight
        other = pltpu.roll(value, SPAN // 2, 1)
        for slot in (REACH, SIDE):
            moved[slot, 0, at, :] = value
            moved[slot, 1, at, :] = other
        moved[SIDE + 1, 0, at, :] = 0.5 * value
        moved[SIDE + 1, 1, at, :] = 0.5 * value
        for offset in range(1, REACH + 1):
            c = phase_ref[REACH + offset - 1, 0, q : q + 1, :]
            s = phase_ref[REACH + offset - 1, 1, q : q + 1, :]
            vc, os, oc, vs = value * c, other * s, other * c, value * s
            moved[REACH + offset, 0, at, :] = vc + os
            moved[REACH + offset, 1, at, :] = oc - vs
            moved[REACH - offset, 0, at, :] = vc - os
            moved[REACH - offset, 1, at, :] = oc + vs

    both = 2 * count_img

    def feature_tile(tile, carry):
        slot = lax.div(tile, REACH)
        entry = lax.rem(tile, REACH) + REACH * (lax.div(tile, REACH * SIDE)) + REACH * lax.div(
            tile, TILES - 1
        )
        start = pl.multiple_of(tile * both, both)

        def load(q):
            at = slice(q * count_img, (q + 1) * count_img)
            a = moved[slot, 0, at, :] * phase_ref[entry, 0, q : q + 1, :]
            b = moved[slot, 1, at, :] * phase_ref[entry, 1, q : q + 1, :]
            return jnp.concatenate([a + b, a - b], axis=0).astype(bf16).astype(f32)

        for j, pair in enumerate(dft36(load)):
            for part, value in enumerate(pair):
                high, low = split(value)
                at = slice(part * SPAN, (part + 1) * SPAN)
                fhi[j, pl.ds(start, both), at] = high
                flo[j, pl.ds(start, both), at] = low
        return carry

    early = TILES * 3 // 5
    lax.fori_loop(0, early, feature_tile, 0)
    for offset in range(1, half):
        source = 2 * behind(offset) + core
        far[offset - 1].wait_recv()
        copy = remote(
            got.at[source], got.at[source], near_send.at[offset], near_recv.at[offset], partner
        )
        copy.start()
        near.append(copy)
    lax.fori_loop(early, TILES, feature_tile, 0)
    for j in range(PAIRS):
        xs[j, :, SPAN * 3 :] = jnp.zeros((2 * rows, xs.shape[2] - SPAN * 3), f32)
    for offset in range(half):
        near[offset].wait_recv()

    for h in range(halves):
        for b in range(padded // LANES):
            block = jnp.concatenate(
                [
                    got[g * halves + h][:, b * LANES : (b + 1) * LANES].astype(f32)
                    for g in range(SPAN // group_rows)
                ],
                axis=0,
            )
            flat[h, b * LANES : (b + 1) * LANES, :] = block.T

    def row_of(q):
        return q // turns, (q % turns) * rows

    power = jnp.zeros((rows, SPAN), f32)
    for q in range(ROT):
        h, start = row_of(q)
        block = flat[h, start : start + rows, :]
        power = power + block * block
    unit = 16

    def refs_tile(tile, carry):
        first = pl.multiple_of(tile * unit, unit)

        def load(q):
            h, start = row_of(q)
            return flat[h, pl.ds(start + first, unit), :]

        low_at = 2 * rows
        for j, (re, im) in enumerate(dft36(load)):
            scale = 1.0 / ROT if j == 0 else 2.0 / ROT
            re, im = scale * re, scale * im
            grid = [[re, im], [-im, re]]
            if j == 0:
                zero = jnp.zeros_like(re)
                grid = [[re, zero], [zero, im]]
            for r in range(2):
                for c in range(2):
                    high, low = split(grid[r][c])
                    at = slice(c * SPAN, (c + 1) * SPAN)
                    rhat[j, pl.ds(first + r * rows, unit), at] = high
                    rhat[j, pl.ds(first + r * rows + low_at, unit), at] = low
        return carry

    lax.fori_loop(0, rows // unit, refs_tile, 0)
    quad = 0.5 * lax.dot_general(
        power, shell_w, (((1,), (1,)), ((), ())), precision=EXACT, preferred_element_type=f32
    )

    def cross_step(j, carry):
        wide = lax.dot_general(
            rhat[j], fhi[j], (((1,), (1,)), ((), ())), preferred_element_type=f32
        )
        rest = lax.dot_general(
            rhat[j, : 2 * rows, :], flo[j], (((1,), (1,)), ((), ())), preferred_element_type=f32
        )
        xs[j, :, :count_n] = wide[: 2 * rows] + wide[2 * rows :] + rest
        return carry

    lax.fori_loop(0, PAIRS, cross_step, 0)

    lane_tiles = xs.shape[2] // LANES
    row_tiles = rows // 8
    used = SHIFTS * count_img
    for k in range(row_tiles):
        for t in range(lane_tiles):
            at = (0, slice(k * 8, (k + 1) * 8), slice(t * LANES, (t + 1) * LANES))
            value = xs[at] - quad[k * 8 : (k + 1) * 8, :]
            if (t + 1) * LANES > used:
                lane = lax.broadcasted_iota(jnp.int32, (8, LANES), 1)
                value = jnp.where(lane < used - t * LANES, value, -BIG)
            xs[at] = value

    def place_of(tile):
        k = pl.multiple_of(lax.div(tile, lane_tiles) * 8, 8)
        t = pl.multiple_of(lax.rem(tile, lane_tiles) * LANES, LANES)
        return k, t

    def load_pairs(k, t):
        return [
            tuple(xs[j, pl.ds(k + part * rows, 8), pl.ds(t, LANES)] for part in range(2))
            for j in range(PAIRS)
        ]

    def score_tile(tile, best):
        k, t = place_of(tile)
        values = idft36(load_pairs(k, t))
        for q, value in enumerate(values):
            xs[q // 2, pl.ds(k + q % 2 * rows, 8), pl.ds(t, LANES)] = value
            best = jnp.maximum(best, value)
        return best

    tiles = row_tiles * lane_tiles
    best = lax.fori_loop(0, tiles, score_tile, jnp.full((8, LANES), -BIG, f32))

    def fold(value, combine):
        reach = count_img
        while reach < LANES:
            value = combine(value, pltpu.roll(value, reach, 1))
            reach *= 2
        return jnp.concatenate([value] * 8, axis=0)

    top = fold(jnp.max(best, axis=0, keepdims=True), jnp.maximum)

    def exp_tile(tile, total):
        k, t = place_of(tile)
        scores = load_pairs(k, t)
        pairs = dft36(lambda q: jnp.exp(scores[q // 2][q % 2] - top))
        for j, pair in enumerate(pairs):
            for part, value in enumerate(pair):
                xs[j, pl.ds(k + part * rows, 8), pl.ds(t, LANES)] = value
        return total + pairs[0][0]

    total = lax.fori_loop(0, tiles, exp_tile, jnp.zeros((8, LANES), f32))
    norm = fold(jnp.sum(total, axis=0, keepdims=True), jnp.add)
    scale = 1.0 / norm
    scale_row = jnp.concatenate([scale[:1]] * lane_tiles, axis=1)

    occupancy = jnp.concatenate(
        [
            sum(
                xs[0, k * 8 : (k + 1) * 8, t * LANES : (t + 1) * LANES] for t in range(lane_tiles)
            )
            * scale
            for k in range(row_tiles)
        ],
        axis=0,
    )
    field = jnp.dot(occupancy, shell_w, precision=EXACT, preferred_element_type=f32)
    high = field.astype(bf16).astype(f32)
    first_lane = lax.rem(lax.broadcasted_iota(jnp.int32, (rows, SPAN), 1), STEP) == 0
    field = jnp.where(first_lane, high, field - high)

    def products(j):
        left = (xs[j] * scale_row).astype(bf16)
        return jnp.dot(left[:, :count_n], fhi[j], preferred_element_type=f32)

    both_real = products(0)
    numh[0, :rows] = 0.5 * both_real[:rows, :SPAN]
    numh[0, rows:] = 0.5 * both_real[rows:, SPAN:]

    def back_step(j, carry):
        value = products(j)
        numh[j, :rows] = value[:rows, :SPAN] + value[rows:, SPAN:]
        numh[j, rows:] = value[:rows, SPAN:] - value[rows:, :SPAN]
        return carry

    lax.fori_loop(1, PAIRS, back_step, 0)

    def number_tile(tile, carry):
        k = pl.multiple_of(tile * 8, 8)
        pairs = [
            tuple(numh[j, pl.ds(k + part * rows, 8), :] for part in range(2)) for j in range(PAIRS)
        ]
        for q, value in enumerate(idft36(pairs)):
            h, start = row_of(q)
            flat[h, pl.ds(start + k, 8), :] = value
        return carry

    lax.fori_loop(0, row_tiles, number_tile, 0)
    for h in range(halves):
        flat[h, width : width + rows, :] = field
        if padded > width + rows:
            flat[h, width + rows :, :] = jnp.zeros((padded - width - rows, SPAN), f32)
        for b in range(padded // LANES):
            block = flat[h, b * LANES : (b + 1) * LANES, :].T
            for g in range(SPAN // group_rows):
                cols_t[h, g, :, b * LANES : (b + 1) * LANES] = block[
                    g * group_rows : (g + 1) * group_rows
                ]

    def block_for(device):
        return cols_t[lax.rem(device, halves), lax.div(device, halves)]

    pairs = []
    for offset in [*range(1, half), 0]:
        slot = ahead(offset)
        pay[offset] = block_for(2 * slot + 1 - core).astype(bf16)
        copy = remote(
            pay.at[offset], mid.at[offset], pair_send.at[offset], pair_recv.at[offset], partner
        )
        copy.start()
        pairs.append(copy)

    lasts = []
    for index, offset in enumerate([*range(1, half), 0]):
        own = block_for(2 * ahead(offset) + core)
        pairs[index].wait_recv()
        value = own + mid[offset].astype(f32)
        if offset:
            mixed[offset] = value.astype(bf16)
            copy = remote(
                mixed.at[offset],
                final.at[offset],
                last_send.at[offset],
                last_recv.at[offset],
                2 * ahead(offset) + core,
            )
            copy.start()
            lasts.append(copy)
        else:
            result = value
    for index, copy in enumerate(lasts):
        copy.wait_recv()
        result = result + final[index + 1].astype(f32)
    weights = result[:, width : width + rows]
    for i in range(pieces):
        inverse = weights[i * STEP : i * STEP + 1] + weights[i * STEP + 1 : i * STEP + 2] + 1.0
        inverse = (2.0 / ROT) / inverse
        for q in range(turns):
            fin[i * piece + q * STEP : i * piece + (q + 1) * STEP, :] = (
                result[i * STEP : (i + 1) * STEP, q * rows : (q + 1) * rows] * inverse
            )
    out_ref[...] = fin[...].T
    for copy in far + near + pairs + lasts:
        copy.wait_send()


def on_device(images, class_refs, sigma2, ctf_group, defocus_bin):
    count_dev = lax.axis_size("img")
    half = count_dev // 2
    count_img = images.shape[0]
    share = class_refs.shape[1]
    piece, halves, pieces, turns, width, padded = geometry(share)
    group_rows = STEP * pieces
    count_n = (SHIFTS + 1) * count_img
    cols = -(-count_n // LANES) * LANES
    travel = pltpu.VMEM((half, group_rows, padded), jnp.bfloat16)
    return pl.pallas_call(
        lambda *refs: em_kernel(count_dev, *refs),
        out_shape=jax.ShapeDtypeStruct(class_refs.shape, jnp.float32),
        in_specs=[pl.BlockSpec(memory_space=pltpu.VMEM)] * 8,
        out_specs=pl.BlockSpec(memory_space=pltpu.VMEM),
        scratch_shapes=[
            pltpu.VMEM((WIDTH, count_img), jnp.float32),
            pltpu.VMEM((SLOTS, 2, ROT * count_img, SPAN), jnp.float32),
            pltpu.VMEM((PAIRS, count_n, 2 * SPAN), jnp.bfloat16),
            pltpu.VMEM((PAIRS, count_n, 2 * SPAN), jnp.bfloat16),
            pltpu.VMEM((PAIRS, 4 * CLASSES, 2 * SPAN), jnp.bfloat16),
            pltpu.VMEM((PAIRS, 2 * CLASSES, cols), jnp.float32),
            pltpu.VMEM((PAIRS, 2 * CLASSES, SPAN), jnp.float32),
            pltpu.VMEM((halves, padded, SPAN), jnp.float32),
            pltpu.VMEM((halves, SPAN // group_rows, group_rows, padded), jnp.float32),
            pltpu.VMEM((share, CLASSES), jnp.float32),
            pltpu.VMEM((group_rows, padded), jnp.bfloat16),
            pltpu.VMEM((count_dev, group_rows, padded), jnp.bfloat16),
            travel,
            travel,
            travel,
            travel,
        ]
        + [pltpu.SemaphoreType.DMA((half,))] * 8,
        compiler_params=pltpu.CompilerParams(
            vmem_limit_bytes=60 * 2**20, collective_id=0, has_side_effects=True
        ),
        name="em_step",
    )(
        images,
        class_refs,
        sigma2,
        ctf_group.reshape(1, count_img),
        defocus_bin.reshape(1, count_img),
        jnp.asarray(ctf_lanes()),
        jnp.asarray(phase_parts()),
        jnp.asarray(channel_order(), dtype=jnp.bfloat16),
    )


def solution(mesh):
    in_specs = (
        P(("groups", "img"), None),
        P("groups", "img"),
        P("groups", None),
        P(("groups", "img")),
        P(("groups", "img")),
    )
    out_specs = P("groups", "img")
    return jax.shard_map(
        on_device, mesh=mesh, in_specs=in_specs, out_specs=out_specs, check_vma=False
    )
```

```python
import math

import jax
import jax.numpy as jnp
import numpy as np
from jax import lax
from jax.experimental import pallas as pl
from jax.experimental.pallas import tpu as pltpu
from jax.sharding import PartitionSpec as P

CLASSES = 48
ROT = 36
SHELLS = 16
ANG = 144
REACH = 3
SHIFTS = 49
BINS = 32
NGROUP = 16

LANES = 128
PARTS = 2 * SHELLS
STEP = ANG // ROT
SPAN = STEP * PARTS
WIDTH = ROT * SPAN
SIDE = 2 * REACH + 1
PAIRS = ROT // 2
TILES = (SHIFTS + 1) // 2
SLOTS = SIDE + 2
BIG = 1e30
LOG2E = math.log2(math.e)
EXACT = lax.Precision.HIGHEST


def phase_parts():
    angles = 2.0 * np.pi * np.arange(ANG) / ANG
    radius = (np.arange(SHELLS) + 1.0) / (2.0 * SHELLS)
    tables = []
    for direction in (np.sin(angles), np.cos(angles)):
        for offset in range(1, REACH + 1):
            phase = 2.0 * np.pi * offset * direction[None, :] * radius[:, None]
            both = []
            for cosine, sine in ((np.cos(phase), -np.sin(phase)), (np.cos(phase), np.sin(phase))):
                both.append(np.stack([cosine, sine]))
            table = np.stack(both, axis=1)
            table = table.reshape(2, PARTS, ROT, STEP).transpose(0, 2, 1, 3)
            tables.append(table.reshape(2, ROT, SPAN))
    tables.append(np.ones((2, ROT, SPAN)))
    return np.stack(tables).astype(np.float32)


def ctf_lanes():
    radius = (np.arange(SHELLS) + 1.0) / (2.0 * SHELLS)
    defocus = 1.0 + np.arange(BINS) / BINS
    table = -np.sin(80.0 * defocus[:, None] * radius**2 + 0.1)
    return np.tile(np.repeat(table, STEP, axis=1), (1, 2)).astype(np.float32)


COS9 = [math.cos(2.0 * math.pi * k / 9.0) for k in range(5)]
SIN9 = [math.sin(2.0 * math.pi * k / 9.0) for k in range(5)]


def even9(first, s1, s2, s3, s4):
    c1, c2 = COS9[1], COS9[2]
    a, b = s1 - s4, s2 - s4
    g1 = c1 * a + c2 * b
    g2 = c2 * (a - b) - c1 * b
    t = s1 + s2 + s4
    w = first + s3
    u = first - 0.5 * s3
    return [w + t, u + g1, u + g2, w - 0.5 * t, u - (g1 + g2)]


def odd9(d1, d2, d3, d4):
    n1, n3, n4 = SIN9[1], SIN9[3], SIN9[4]
    a, b, c = d1 + d2, d2 + d4, d1 - d4
    h1 = n1 * a + n4 * b
    h2 = n1 * c + n4 * a
    e = n3 * d3
    return [h1 + e, h2 - e, n3 * (d1 - d2 + d4), h2 - h1 + e]


def where_q(a, b):
    return (9 * a + 4 * b) % ROT


def dft36(load):
    parts = []
    for a in range(4):
        x = [load(where_q(a, b)) for b in range(9)]
        s = [x[j] + x[9 - j] for j in range(1, 5)]
        d = [x[9 - j] - x[j] for j in range(1, 5)]
        parts.append((even9(x[0], *s), [None] + odd9(*d)))
    y = [part[0][0] for part in parts]
    p, m = y[0] + y[2], y[1] + y[3]
    pairs = [(p + m, p - m), (y[0] - y[2], y[3] - y[1])]
    for g in range(1, 5):
        re = [part[0][g] for part in parts]
        im = [part[1][g] for part in parts]
        rp, rm, ip, im_ = re[0] + re[2], re[0] - re[2], im[0] + im[2], im[0] - im[2]
        sp, sm, jp, jm = re[1] + re[3], re[1] - re[3], im[1] + im[3], im[1] - im[3]
        pairs.append((rp + sp, ip + jp))
        pairs.append((rm + jm, im_ - sm))
        pairs.append((rp - sp, ip - jp))
        pairs.append((rm - jm, im_ + sm))
    return pairs


def idft36(pairs):
    p, m = pairs[0][0] + pairs[0][1], pairs[0][0] - pairs[0][1]
    re, im = pairs[1]
    parts = [[(p + re, None)], [(m - im, None)], [(p - re, None)], [(m + im, None)]]
    for g in range(4):
        (r0, i0), (r1, i1), (r2, i2), (r3, i3) = pairs[2 + 4 * g : 6 + 4 * g]
        rp, rm, ip, im_ = r0 + r2, r0 - r2, i0 + i2, i0 - i2
        sp, sm, jp, jm = r1 + r3, r1 - r3, i1 + i3, i1 - i3
        parts[0].append((rp + sp, ip + jp))
        parts[1].append((rm - jm, im_ + sm))
        parts[2].append((rp - sp, ip - jp))
        parts[3].append((rm + jm, im_ - sm))
    out = [None] * ROT
    for a in range(4):
        y = parts[a]
        even = even9(y[0][0], y[1][0], y[2][0], y[3][0], y[4][0])
        odd = [None] + odd9(y[1][1], y[2][1], y[3][1], y[4][1])
        out[where_q(a, 0)] = even[0]
        for b in range(1, 5):
            out[where_q(a, b)] = even[b] - odd[b]
            out[where_q(a, 9 - b)] = even[b] + odd[b]
    return out


def split(value):
    high = value.astype(jnp.bfloat16)
    return high, (value - high.astype(jnp.float32)).astype(jnp.bfloat16)


def image_blocks(img_ref):
    count = img_ref.shape[0]
    lane = lax.broadcasted_iota(jnp.int32, (count, LANES), 1)
    source = [
        img_ref[:, v * LANES : (v + 1) * LANES].astype(jnp.float32)
        for v in range(img_ref.shape[1] // LANES)
    ]
    per = LANES // STEP
    rows = []
    for p in range(PARTS):
        v, shift = divmod(p * ANG, LANES)
        value = source[v]
        if shift:
            value = jnp.where(
                lane < LANES - shift,
                pltpu.roll(source[v], LANES - shift, 1),
                pltpu.roll(source[v + 1], LANES - shift, 1),
            )
        rows.append(value)
    reach = 1
    while reach < per:
        low = (lane & (reach * STEP)) == 0
        new = list(rows)
        for p in range(per):
            if not p & reach:
                first, second = rows[p], rows[p + reach]
                new[p] = jnp.where(low, first, pltpu.roll(second, reach * STEP, 1))
                new[p + reach] = jnp.where(
                    low, pltpu.roll(first, LANES - reach * STEP, 1), second
                )
        rows = new
        reach *= 2
    for q in range(per, ROT):
        value = None
        for p in range(PARTS):
            v, start = divmod(p * ANG + q * STEP, LANES)
            moved = pltpu.roll(source[v], (p * STEP - start) % LANES, 1)
            if value is None:
                value = moved
            else:
                value = jnp.where(lane < p * STEP, value, moved)
        rows.append(value)
    return rows


def geometry(share):
    piece = min(share, ANG)
    halves = ANG // piece
    pieces = share // piece
    turns = piece // STEP
    width = turns * CLASSES
    padded = -(-(width + CLASSES) // LANES) * LANES
    return piece, halves, pieces, turns, width, padded


def em_kernel(
    count_dev,
    img_ref,
    refs_ref,
    sigma_ref,
    group_ref,
    bin_ref,
    ctf_ref,
    phase_ref,
    out_ref,
    moved,
    fhi,
    flo,
    rhat,
    xs,
    numh,
    flat,
    cols_t,
    fin,
    mine,
    got,
    pay,
    mid,
    mixed,
    final,
    near_send,
    near_recv,
    far_send,
    far_recv,
    pair_send,
    pair_recv,
    last_send,
    last_recv,
):
    rows = CLASSES
    count_img = img_ref.shape[0]
    share = refs_ref.shape[1]
    piece, halves, pieces, turns, width, padded = geometry(share)
    group_rows = STEP * pieces
    count_n = fhi.shape[2]
    half = count_dev // 2
    me = lax.axis_index("img")
    core = lax.rem(me, 2)
    place = lax.div(me, 2)
    partner = me + 1 - 2 * core
    f32, bf16 = jnp.float32, jnp.bfloat16

    def ahead(offset):
        return lax.rem(place + offset, half)

    def behind(offset):
        return lax.rem(place + half - offset, half)

    barrier = pltpu.get_barrier_semaphore()
    for offset in range(1, half):
        pl.semaphore_signal(
            barrier,
            inc=1,
            device_id={"img": 2 * ahead(offset) + core},
            device_id_type=pl.DeviceIdType.MESH,
        )
    pl.semaphore_signal(
        barrier, inc=1, device_id={"img": partner}, device_id_type=pl.DeviceIdType.MESH
    )

    def remote(source, target, send, recv, device):
        return pltpu.make_async_remote_copy(
            src_ref=source,
            dst_ref=target,
            send_sem=send,
            recv_sem=recv,
            device_id={"img": device},
            device_id_type=pl.DeviceIdType.MESH,
        )

    fin[...] = refs_ref[...].astype(f32).T
    turned = []
    for q in range(turns):
        turned.append(
            jnp.concatenate(
                [fin[i * piece + q * STEP : i * piece + (q + 1) * STEP, :] for i in range(pieces)],
                axis=0,
            )
        )
    turned.append(jnp.zeros((group_rows, padded - width), f32))
    own = jnp.concatenate(turned, axis=1).astype(bf16)
    mine[...] = own
    got[me] = own
    pl.semaphore_wait(barrier, half)

    far = [
        remote(
            mine,
            got.at[me],
            far_send.at[offset],
            far_recv.at[offset],
            2 * ahead(offset) + core,
        )
        for offset in range(1, half)
    ]
    near = [remote(mine, got.at[me], near_send.at[0], near_recv.at[0], partner)]
    for copy in far + near:
        copy.start()

    blocks = image_blocks(img_ref)

    def pick(ids, table):
        hot = ids == lax.broadcasted_iota(jnp.int32, (table.shape[0], count_img), 0)
        return lax.dot_general(
            hot.astype(f32),
            table,
            (((0,), (0,)), ((), ())),
            precision=EXACT,
            preferred_element_type=f32,
        )

    lane_shell = lax.rem(
        lax.div(lax.broadcasted_iota(jnp.int32, (SHELLS, SPAN), 1), STEP), SHELLS
    )
    spread = (lane_shell == lax.broadcasted_iota(jnp.int32, (SHELLS, SPAN), 0)).astype(f32)
    noise = jnp.dot(
        pick(group_ref[...], sigma_ref[...]), spread, precision=EXACT, preferred_element_type=f32
    )
    ctf = pick(bin_ref[...], ctf_ref[...])
    weight = ctf / noise
    shell_w = jnp.concatenate([ctf * ctf / noise] * (LANES // count_img), axis=0)

    for q in range(ROT):
        at = slice(q * count_img, (q + 1) * count_img)
        value = blocks[q] * weight
        other = pltpu.roll(value, SPAN // 2, 1)
        for slot in (REACH, SIDE):
            moved[slot, 0, at, :] = value
            moved[slot, 1, at, :] = other
        moved[SIDE + 1, 0, at, :] = 0.5 * value
        moved[SIDE + 1, 1, at, :] = 0.5 * value
        for offset in range(1, REACH + 1):
            c = phase_ref[REACH + offset - 1, 0, q : q + 1, :]
            s = phase_ref[REACH + offset - 1, 1, q : q + 1, :]
            vc, os, oc, vs = value * c, other * s, other * c, value * s
            moved[REACH + offset, 0, at, :] = vc + os
            moved[REACH + offset, 1, at, :] = oc - vs
            moved[REACH - offset, 0, at, :] = vc - os
            moved[REACH - offset, 1, at, :] = oc + vs

    both = 2 * count_img

    def feature_tile(tile, carry):
        slot = lax.div(tile, REACH)
        entry = lax.rem(tile, REACH) + REACH * (lax.div(tile, REACH * SIDE)) + REACH * lax.div(
            tile, TILES - 1
        )
        start = pl.multiple_of(tile * both, both)

        def load(q):
            at = slice(q * count_img, (q + 1) * count_img)
            a = moved[slot, 0, at, :] * phase_ref[entry, 0, q : q + 1, :]
            b = moved[slot, 1, at, :] * phase_ref[entry, 1, q : q + 1, :]
            return jnp.concatenate([a + b, a - b], axis=0).astype(bf16).astype(f32)

        for j, pair in enumerate(dft36(load)):
            for part, value in enumerate(pair):
                high, low = split(value)
                fhi[j, part, pl.ds(start, both), :] = high
                flo[j, part, pl.ds(start, both), :] = low
        return carry

    early = TILES * 3 // 5
    lax.fori_loop(0, early, feature_tile, 0)
    for offset in range(1, half):
        source = 2 * behind(offset) + core
        far[offset - 1].wait_recv()
        copy = remote(
            got.at[source], got.at[source], near_send.at[offset], near_recv.at[offset], partner
        )
        copy.start()
        near.append(copy)
    lax.fori_loop(early, TILES, feature_tile, 0)
    for j in range(PAIRS):
        xs[j, :, SPAN * 3 :] = jnp.zeros((2 * rows, xs.shape[2] - SPAN * 3), f32)
    for offset in range(half):
        near[offset].wait_recv()

    for h in range(halves):
        for b in range(padded // LANES):
            block = jnp.concatenate(
                [
                    got[g * halves + h][:, b * LANES : (b + 1) * LANES].astype(f32)
                    for g in range(SPAN // group_rows)
                ],
                axis=0,
            )
            flat[h, b * LANES : (b + 1) * LANES, :] = block.T

    def row_of(q):
        return q // turns, (q % turns) * rows

    power = jnp.zeros((rows, SPAN), f32)
    for q in range(ROT):
        h, start = row_of(q)
        block = flat[h, start : start + rows, :]
        power = power + block * block
    unit = 16

    def refs_tile(tile, carry):
        first = pl.multiple_of(tile * unit, unit)

        def load(q):
            h, start = row_of(q)
            return flat[h, pl.ds(start + first, unit), :]

        low_at = 2 * rows
        for j, (re, im) in enumerate(dft36(load)):
            scale = LOG2E / ROT if j == 0 else 2.0 * LOG2E / ROT
            re, im = scale * re, scale * im
            grid = [[re, im], [-im, re]]
            if j == 0:
                zero = jnp.zeros_like(re)
                grid = [[re, zero], [zero, im]]
            for r in range(2):
                for c in range(2):
                    high, low = split(grid[r][c])
                    rhat[j, c, pl.ds(first + r * rows, unit), :] = high
                    rhat[j, c, pl.ds(first + r * rows + low_at, unit), :] = low
        return carry

    lax.fori_loop(0, rows // unit, refs_tile, 0)
    quad = 0.5 * LOG2E * lax.dot_general(
        power, shell_w, (((1,), (1,)), ((), ())), precision=EXACT, preferred_element_type=f32
    )

    def both_halves(ref, j):
        return jnp.concatenate([ref[j, 0], ref[j, 1]], axis=1)

    def cross_step(j, carry):
        left = both_halves(rhat, j)
        wide = lax.dot_general(
            left, both_halves(fhi, j), (((1,), (1,)), ((), ())), preferred_element_type=f32
        )
        rest = lax.dot_general(
            left[: 2 * rows],
            both_halves(flo, j),
            (((1,), (1,)), ((), ())),
            preferred_element_type=f32,
        )
        xs[j, :, :count_n] = wide[: 2 * rows] + wide[2 * rows :] + rest
        return carry

    lax.fori_loop(0, PAIRS, cross_step, 0, unroll=True)

    lane_tiles = xs.shape[2] // LANES
    row_tiles = rows // 8
    used = SHIFTS * count_img
    for k in range(row_tiles):
        for t in range(lane_tiles):
            at = (0, slice(k * 8, (k + 1) * 8), slice(t * LANES, (t + 1) * LANES))
            value = xs[at] - quad[k * 8 : (k + 1) * 8, :]
            if (t + 1) * LANES > used:
                lane = lax.broadcasted_iota(jnp.int32, (8, LANES), 1)
                value = jnp.where(lane < used - t * LANES, value, -BIG)
            xs[at] = value

    def place_of(tile):
        k = pl.multiple_of(lax.div(tile, lane_tiles) * 8, 8)
        t = pl.multiple_of(lax.rem(tile, lane_tiles) * LANES, LANES)
        return k, t

    def load_pairs(k, t):
        return [
            tuple(xs[j, pl.ds(k + part * rows, 8), pl.ds(t, LANES)] for part in range(2))
            for j in range(PAIRS)
        ]

    def score_tile(tile, best):
        k, t = place_of(tile)
        values = idft36(load_pairs(k, t))
        for q, value in enumerate(values):
            xs[q // 2, pl.ds(k + q % 2 * rows, 8), pl.ds(t, LANES)] = value
            best = jnp.maximum(best, value)
        return best

    tiles = row_tiles * lane_tiles
    best = lax.fori_loop(0, tiles, score_tile, jnp.full((8, LANES), -BIG, f32))

    def fold(value, combine):
        reach = count_img
        while reach < LANES:
            value = combine(value, pltpu.roll(value, reach, 1))
            reach *= 2
        return jnp.concatenate([value] * 8, axis=0)

    top = fold(jnp.max(best, axis=0, keepdims=True), jnp.maximum)

    def exp_tile(tile, total):
        k, t = place_of(tile)
        scores = load_pairs(k, t)
        pairs = dft36(lambda q: jnp.exp2(scores[q // 2][q % 2] - top))
        for j, pair in enumerate(pairs):
            for part, value in enumerate(pair):
                xs[j, pl.ds(k + part * rows, 8), pl.ds(t, LANES)] = value
        return total + pairs[0][0]

    total = lax.fori_loop(0, tiles, exp_tile, jnp.zeros((8, LANES), f32))
    norm = fold(jnp.sum(total, axis=0, keepdims=True), jnp.add)
    scale = 1.0 / norm
    scale_row = jnp.concatenate([scale[:1]] * lane_tiles, axis=1)

    occupancy = jnp.concatenate(
        [
            sum(
                xs[0, k * 8 : (k + 1) * 8, t * LANES : (t + 1) * LANES] for t in range(lane_tiles)
            )
            * scale
            for k in range(row_tiles)
        ],
        axis=0,
    )
    field = jnp.dot(occupancy, shell_w, precision=EXACT, preferred_element_type=f32)
    high = field.astype(bf16).astype(f32)
    first_lane = lax.rem(lax.broadcasted_iota(jnp.int32, (rows, SPAN), 1), STEP) == 0
    field = jnp.where(first_lane, high, field - high)

    def products(j):
        left = (xs[j] * scale_row).astype(bf16)
        return jnp.dot(left[:, :count_n], both_halves(fhi, j), preferred_element_type=f32)

    both_real = products(0)
    numh[0, :rows] = 0.5 * both_real[:rows, :SPAN]
    numh[0, rows:] = 0.5 * both_real[rows:, SPAN:]

    def back_step(j, carry):
        value = products(j)
        numh[j, :rows] = value[:rows, :SPAN] + value[rows:, SPAN:]
        numh[j, rows:] = value[:rows, SPAN:] - value[rows:, :SPAN]
        return carry

    lax.fori_loop(1, PAIRS, back_step, 0, unroll=True)

    def number_tile(tile, carry):
        k = pl.multiple_of(tile * 8, 8)
        pairs = [
            tuple(numh[j, pl.ds(k + part * rows, 8), :] for part in range(2)) for j in range(PAIRS)
        ]
        for q, value in enumerate(idft36(pairs)):
            h, start = row_of(q)
            flat[h, pl.ds(start + k, 8), :] = value
        return carry

    lax.fori_loop(0, row_tiles, number_tile, 0)
    for h in range(halves):
        flat[h, width : width + rows, :] = field
        if padded > width + rows:
            flat[h, width + rows :, :] = jnp.zeros((padded - width - rows, SPAN), f32)
        for b in range(padded // LANES):
            block = flat[h, b * LANES : (b + 1) * LANES, :].T
            for g in range(SPAN // group_rows):
                cols_t[h, g, :, b * LANES : (b + 1) * LANES] = block[
                    g * group_rows : (g + 1) * group_rows
                ]

    def block_for(device):
        return cols_t[lax.rem(device, halves), lax.div(device, halves)]

    pairs = []
    for offset in [*range(1, half), 0]:
        slot = ahead(offset)
        pay[offset] = block_for(2 * slot + 1 - core).astype(bf16)
        copy = remote(
            pay.at[offset], mid.at[offset], pair_send.at[offset], pair_recv.at[offset], partner
        )
        copy.start()
        pairs.append(copy)

    lasts = []
    for index, offset in enumerate([*range(1, half), 0]):
        own = block_for(2 * ahead(offset) + core)
        pairs[index].wait_recv()
        value = own + mid[offset].astype(f32)
        if offset:
            mixed[offset] = value.astype(bf16)
            copy = remote(
                mixed.at[offset],
                final.at[offset],
                last_send.at[offset],
                last_recv.at[offset],
                2 * ahead(offset) + core,
            )
            copy.start()
            lasts.append(copy)
        else:
            result = value
    for index, copy in enumerate(lasts):
        copy.wait_recv()
        result = result + final[index + 1].astype(f32)
    weights = result[:, width : width + rows]
    for i in range(pieces):
        inverse = weights[i * STEP : i * STEP + 1] + weights[i * STEP + 1 : i * STEP + 2] + 1.0
        inverse = (2.0 / ROT) / inverse
        for q in range(turns):
            fin[i * piece + q * STEP : i * piece + (q + 1) * STEP, :] = (
                result[i * STEP : (i + 1) * STEP, q * rows : (q + 1) * rows] * inverse
            )
    out_ref[...] = fin[...].T
    for copy in far + near + pairs + lasts:
        copy.wait_send()


def on_device(images, class_refs, sigma2, ctf_group, defocus_bin):
    count_dev = lax.axis_size("img")
    half = count_dev // 2
    count_img = images.shape[0]
    share = class_refs.shape[1]
    piece, halves, pieces, turns, width, padded = geometry(share)
    group_rows = STEP * pieces
    count_n = (SHIFTS + 1) * count_img
    cols = -(-count_n // LANES) * LANES
    travel = pltpu.VMEM((half, group_rows, padded), jnp.bfloat16)
    return pl.pallas_call(
        lambda *refs: em_kernel(count_dev, *refs),
        out_shape=jax.ShapeDtypeStruct(class_refs.shape, jnp.float32),
        in_specs=[pl.BlockSpec(memory_space=pltpu.VMEM)] * 7,
        out_specs=pl.BlockSpec(memory_space=pltpu.VMEM),
        scratch_shapes=[
            pltpu.VMEM((SLOTS, 2, ROT * count_img, SPAN), jnp.float32),
            pltpu.VMEM((PAIRS, 2, count_n, SPAN), jnp.bfloat16),
            pltpu.VMEM((PAIRS, 2, count_n, SPAN), jnp.bfloat16),
            pltpu.VMEM((PAIRS, 2, 4 * CLASSES, SPAN), jnp.bfloat16),
            pltpu.VMEM((PAIRS, 2 * CLASSES, cols), jnp.float32),
            pltpu.VMEM((PAIRS, 2 * CLASSES, SPAN), jnp.float32),
            pltpu.VMEM((halves, padded, SPAN), jnp.float32),
            pltpu.VMEM((halves, SPAN // group_rows, group_rows, padded), jnp.float32),
            pltpu.VMEM((share, CLASSES), jnp.float32),
            pltpu.VMEM((group_rows, padded), jnp.bfloat16),
            pltpu.VMEM((count_dev, group_rows, padded), jnp.bfloat16),
            travel,
            travel,
            travel,
            travel,
        ]
        + [pltpu.SemaphoreType.DMA((half,))] * 8,
        compiler_params=pltpu.CompilerParams(
            vmem_limit_bytes=60 * 2**20, collective_id=0, has_side_effects=True
        ),
        name="em_step",
    )(
        images,
        class_refs,
        sigma2,
        ctf_group.reshape(1, count_img),
        defocus_bin.reshape(1, count_img),
        jnp.asarray(ctf_lanes()),
        jnp.asarray(phase_parts()),
    )


def solution(mesh):
    in_specs = (
        P(("groups", "img"), None),
        P("groups", "img"),
        P("groups", None),
        P(("groups", "img")),
        P(("groups", "img")),
    )
    out_specs = P("groups", "img")
    return jax.shard_map(
        on_device, mesh=mesh, in_specs=in_specs, out_specs=out_specs, check_vma=False
    )
```

```python
import math

import jax
import jax.numpy as jnp
import numpy as np
from jax import lax
from jax.experimental import pallas as pl
from jax.experimental.pallas import tpu as pltpu
from jax.sharding import PartitionSpec as P

CLASSES = 48
ROT = 36
SHELLS = 16
ANG = 144
REACH = 3
SHIFTS = 49
BINS = 32
NGROUP = 16

LANES = 128
PARTS = 2 * SHELLS
STEP = ANG // ROT
SPAN = STEP * PARTS
WIDTH = ROT * SPAN
SIDE = 2 * REACH + 1
PAIRS = ROT // 2
TILES = (SHIFTS + 1) // 2
SLOTS = SIDE + 2
BIG = 1e30
LOG2E = math.log2(math.e)
EXACT = lax.Precision.HIGHEST


def phase_parts():
    angles = 2.0 * np.pi * np.arange(ANG) / ANG
    radius = (np.arange(SHELLS) + 1.0) / (2.0 * SHELLS)
    tables = []
    for direction in (np.sin(angles), np.cos(angles)):
        for offset in range(1, REACH + 1):
            phase = 2.0 * np.pi * offset * direction[None, :] * radius[:, None]
            both = []
            for cosine, sine in ((np.cos(phase), -np.sin(phase)), (np.cos(phase), np.sin(phase))):
                both.append(np.stack([cosine, sine]))
            table = np.stack(both, axis=1)
            table = table.reshape(2, PARTS, ROT, STEP).transpose(0, 2, 1, 3)
            tables.append(table.reshape(2, ROT, SPAN))
    tables.append(np.ones((2, ROT, SPAN)))
    return np.stack(tables).astype(np.float32)


def ctf_lanes():
    radius = (np.arange(SHELLS) + 1.0) / (2.0 * SHELLS)
    defocus = 1.0 + np.arange(BINS) / BINS
    table = -np.sin(80.0 * defocus[:, None] * radius**2 + 0.1)
    return np.tile(np.repeat(table, STEP, axis=1), (1, 2)).astype(np.float32)


COS9 = [math.cos(2.0 * math.pi * k / 9.0) for k in range(5)]
SIN9 = [math.sin(2.0 * math.pi * k / 9.0) for k in range(5)]


def even9(first, s1, s2, s3, s4):
    c1, c2 = COS9[1], COS9[2]
    a, b = s1 - s4, s2 - s4
    g1 = c1 * a + c2 * b
    g2 = c2 * (a - b) - c1 * b
    t = s1 + s2 + s4
    w = first + s3
    u = first - 0.5 * s3
    return [w + t, u + g1, u + g2, w - 0.5 * t, u - (g1 + g2)]


def odd9(d1, d2, d3, d4):
    n1, n3, n4 = SIN9[1], SIN9[3], SIN9[4]
    a, b, c = d1 + d2, d2 + d4, d1 - d4
    h1 = n1 * a + n4 * b
    h2 = n1 * c + n4 * a
    e = n3 * d3
    return [h1 + e, h2 - e, n3 * (d1 - d2 + d4), h2 - h1 + e]


def where_q(a, b):
    return (9 * a + 4 * b) % ROT


def dft36(load):
    parts = []
    for a in range(4):
        x = [load(where_q(a, b)) for b in range(9)]
        s = [x[j] + x[9 - j] for j in range(1, 5)]
        d = [x[9 - j] - x[j] for j in range(1, 5)]
        parts.append((even9(x[0], *s), [None] + odd9(*d)))
    y = [part[0][0] for part in parts]
    p, m = y[0] + y[2], y[1] + y[3]
    pairs = [(p + m, p - m), (y[0] - y[2], y[3] - y[1])]
    for g in range(1, 5):
        re = [part[0][g] for part in parts]
        im = [part[1][g] for part in parts]
        rp, rm, ip, im_ = re[0] + re[2], re[0] - re[2], im[0] + im[2], im[0] - im[2]
        sp, sm, jp, jm = re[1] + re[3], re[1] - re[3], im[1] + im[3], im[1] - im[3]
        pairs.append((rp + sp, ip + jp))
        pairs.append((rm + jm, im_ - sm))
        pairs.append((rp - sp, ip - jp))
        pairs.append((rm - jm, im_ + sm))
    return pairs


def idft36(pairs):
    p, m = pairs[0][0] + pairs[0][1], pairs[0][0] - pairs[0][1]
    re, im = pairs[1]
    parts = [[(p + re, None)], [(m - im, None)], [(p - re, None)], [(m + im, None)]]
    for g in range(4):
        (r0, i0), (r1, i1), (r2, i2), (r3, i3) = pairs[2 + 4 * g : 6 + 4 * g]
        rp, rm, ip, im_ = r0 + r2, r0 - r2, i0 + i2, i0 - i2
        sp, sm, jp, jm = r1 + r3, r1 - r3, i1 + i3, i1 - i3
        parts[0].append((rp + sp, ip + jp))
        parts[1].append((rm - jm, im_ + sm))
        parts[2].append((rp - sp, ip - jp))
        parts[3].append((rm + jm, im_ - sm))
    out = [None] * ROT
    for a in range(4):
        y = parts[a]
        even = even9(y[0][0], y[1][0], y[2][0], y[3][0], y[4][0])
        odd = [None] + odd9(y[1][1], y[2][1], y[3][1], y[4][1])
        out[where_q(a, 0)] = even[0]
        for b in range(1, 5):
            out[where_q(a, b)] = even[b] - odd[b]
            out[where_q(a, 9 - b)] = even[b] + odd[b]
    return out


def split(value):
    high = value.astype(jnp.bfloat16)
    return high, (value - high.astype(jnp.float32)).astype(jnp.bfloat16)


def image_blocks(img_ref):
    count = img_ref.shape[0]
    lane = lax.broadcasted_iota(jnp.int32, (count, LANES), 1)
    source = [
        img_ref[:, v * LANES : (v + 1) * LANES].astype(jnp.float32)
        for v in range(img_ref.shape[1] // LANES)
    ]
    per = LANES // STEP
    rows = []
    for p in range(PARTS):
        v, shift = divmod(p * ANG, LANES)
        value = source[v]
        if shift:
            value = jnp.where(
                lane < LANES - shift,
                pltpu.roll(source[v], LANES - shift, 1),
                pltpu.roll(source[v + 1], LANES - shift, 1),
            )
        rows.append(value)
    reach = 1
    while reach < per:
        low = (lane & (reach * STEP)) == 0
        new = list(rows)
        for p in range(per):
            if not p & reach:
                first, second = rows[p], rows[p + reach]
                new[p] = jnp.where(low, first, pltpu.roll(second, reach * STEP, 1))
                new[p + reach] = jnp.where(
                    low, pltpu.roll(first, LANES - reach * STEP, 1), second
                )
        rows = new
        reach *= 2
    for q in range(per, ROT):
        value = None
        for p in range(PARTS):
            v, start = divmod(p * ANG + q * STEP, LANES)
            moved = pltpu.roll(source[v], (p * STEP - start) % LANES, 1)
            if value is None:
                value = moved
            else:
                value = jnp.where(lane < p * STEP, value, moved)
        rows.append(value)
    return rows


def tree(combine, values):
    while len(values) > 1:
        joined = [combine(a, b) for a, b in zip(values[::2], values[1::2])]
        values = joined + values[len(joined) * 2 :]
    return values[0]


def geometry(share):
    piece = min(share, ANG)
    halves = ANG // piece
    pieces = share // piece
    turns = piece // STEP
    width = turns * CLASSES
    padded = -(-(width + CLASSES) // LANES) * LANES
    return piece, halves, pieces, turns, width, padded


def em_kernel(
    count_dev,
    img_ref,
    refs_ref,
    sigma_ref,
    group_ref,
    bin_ref,
    ctf_ref,
    phase_ref,
    out_ref,
    moved,
    fhi,
    flo,
    fhi_b,
    flo_b,
    rhat,
    xs,
    xs_b,
    xp,
    quad_ref,
    sums,
    part_sums,
    numh,
    flat,
    cols_t,
    fin,
    mine,
    got,
    pay,
    mid,
    mixed,
    final,
    near_send,
    near_recv,
    far_send,
    far_recv,
    pair_send,
    pair_recv,
    last_send,
    last_recv,
):
    rows = CLASSES
    count_img = img_ref.shape[0]
    share = refs_ref.shape[1]
    piece, halves, pieces, turns, width, padded = geometry(share)
    group_rows = STEP * pieces
    count_a, count_b = fhi.shape[2], fhi_b.shape[2]
    half = count_dev // 2
    me = lax.axis_index("img")
    core = lax.rem(me, 2)
    place = lax.div(me, 2)
    partner = me + 1 - 2 * core
    f32, bf16 = jnp.float32, jnp.bfloat16

    def ahead(offset):
        return lax.rem(place + offset, half)

    def behind(offset):
        return lax.rem(place + half - offset, half)

    barrier = pltpu.get_barrier_semaphore()
    for offset in range(1, half):
        pl.semaphore_signal(
            barrier,
            inc=1,
            device_id={"img": 2 * ahead(offset) + core},
            device_id_type=pl.DeviceIdType.MESH,
        )
    pl.semaphore_signal(
        barrier, inc=1, device_id={"img": partner}, device_id_type=pl.DeviceIdType.MESH
    )

    def remote(source, target, send, recv, device):
        return pltpu.make_async_remote_copy(
            src_ref=source,
            dst_ref=target,
            send_sem=send,
            recv_sem=recv,
            device_id={"img": device},
            device_id_type=pl.DeviceIdType.MESH,
        )

    fin[...] = refs_ref[...].astype(f32).T
    turned = []
    for q in range(turns):
        turned.append(
            jnp.concatenate(
                [fin[i * piece + q * STEP : i * piece + (q + 1) * STEP, :] for i in range(pieces)],
                axis=0,
            )
        )
    turned.append(jnp.zeros((group_rows, padded - width), f32))
    own = jnp.concatenate(turned, axis=1).astype(bf16)
    mine[...] = own
    got[me] = own
    pl.semaphore_wait(barrier, half)

    far = [
        remote(
            mine,
            got.at[me],
            far_send.at[offset],
            far_recv.at[offset],
            2 * ahead(offset) + core,
        )
        for offset in range(1, half)
    ]
    near = [remote(mine, got.at[me], near_send.at[0], near_recv.at[0], partner)]
    for copy in far + near:
        copy.start()

    blocks = image_blocks(img_ref)

    def pick(ids, table):
        hot = ids == lax.broadcasted_iota(jnp.int32, (table.shape[0], count_img), 0)
        return lax.dot_general(
            hot.astype(f32),
            table,
            (((0,), (0,)), ((), ())),
            precision=EXACT,
            preferred_element_type=f32,
        )

    lane_shell = lax.rem(
        lax.div(lax.broadcasted_iota(jnp.int32, (SHELLS, SPAN), 1), STEP), SHELLS
    )
    spread = (lane_shell == lax.broadcasted_iota(jnp.int32, (SHELLS, SPAN), 0)).astype(f32)
    noise = jnp.dot(
        pick(group_ref[...], sigma_ref[...]), spread, precision=EXACT, preferred_element_type=f32
    )
    ctf = pick(bin_ref[...], ctf_ref[...])
    weight = ctf / noise
    shell_w = jnp.concatenate([ctf * ctf / noise] * (LANES // count_img), axis=0)

    for q in range(ROT):
        at = slice(q * count_img, (q + 1) * count_img)
        value = blocks[q] * weight
        other = pltpu.roll(value, SPAN // 2, 1)
        for slot in (REACH, SIDE):
            moved[slot, 0, at, :] = value
            moved[slot, 1, at, :] = other
        moved[SIDE + 1, 0, at, :] = 0.5 * value
        moved[SIDE + 1, 1, at, :] = 0.5 * value
        for offset in range(1, REACH + 1):
            c = phase_ref[REACH + offset - 1, 0, q : q + 1, :]
            s = phase_ref[REACH + offset - 1, 1, q : q + 1, :]
            vc, os, oc, vs = value * c, other * s, other * c, value * s
            moved[REACH + offset, 0, at, :] = vc + os
            moved[REACH + offset, 1, at, :] = oc - vs
            moved[REACH - offset, 0, at, :] = vc - os
            moved[REACH - offset, 1, at, :] = oc + vs

    both = 2 * count_img

    tiles_a = count_a // both

    def feature_tile(tile, high_ref, low_ref, first):
        slot = lax.div(tile, REACH)
        entry = lax.rem(tile, REACH) + REACH * (lax.div(tile, REACH * SIDE)) + REACH * lax.div(
            tile, TILES - 1
        )
        start = pl.multiple_of((tile - first) * both, both)

        def load(q):
            at = slice(q * count_img, (q + 1) * count_img)
            a = moved[slot, 0, at, :] * phase_ref[entry, 0, q : q + 1, :]
            b = moved[slot, 1, at, :] * phase_ref[entry, 1, q : q + 1, :]
            return jnp.concatenate([a + b, a - b], axis=0).astype(bf16).astype(f32)

        for j, pair in enumerate(dft36(load)):
            for part, value in enumerate(pair):
                high, low = split(value)
                high_ref[j, part, pl.ds(start, both), :] = high
                low_ref[j, part, pl.ds(start, both), :] = low

    def feature_tile_a(tile, carry):
        feature_tile(tile, fhi, flo, 0)
        return carry

    early = tiles_a * 5 // 8
    lax.fori_loop(0, early, feature_tile_a, 0)
    for offset in range(1, half):
        source = 2 * behind(offset) + core
        far[offset - 1].wait_recv()
        copy = remote(
            got.at[source], got.at[source], near_send.at[offset], near_recv.at[offset], partner
        )
        copy.start()
        near.append(copy)
    lax.fori_loop(early, tiles_a, feature_tile_a, 0)
    for j in range(PAIRS):
        xs_b[j, :, LANES:] = jnp.zeros((2 * rows, LANES), f32)
    for offset in range(half):
        near[offset].wait_recv()

    for h in range(halves):
        for b in range(padded // LANES):
            block = jnp.concatenate(
                [
                    got[g * halves + h][:, b * LANES : (b + 1) * LANES].astype(f32)
                    for g in range(SPAN // group_rows)
                ],
                axis=0,
            )
            flat[h, b * LANES : (b + 1) * LANES, :] = block.T

    def row_of(q):
        return q // turns, (q % turns) * rows

    power = jnp.zeros((rows, SPAN), f32)
    for q in range(ROT):
        h, start = row_of(q)
        block = flat[h, start : start + rows, :]
        power = power + block * block
    unit = 16

    def refs_tile(tile, carry):
        first = pl.multiple_of(tile * unit, unit)

        def load(q):
            h, start = row_of(q)
            return flat[h, pl.ds(start + first, unit), :]

        low_at = 2 * rows
        for j, (re, im) in enumerate(dft36(load)):
            scale = LOG2E / ROT if j == 0 else 2.0 * LOG2E / ROT
            re, im = scale * re, scale * im
            grid = [[re, im], [-im, re]]
            if j == 0:
                zero = jnp.zeros_like(re)
                grid = [[re, zero], [zero, im]]
            for r in range(2):
                for c in range(2):
                    high, low = split(grid[r][c])
                    rhat[j, c, pl.ds(first + r * rows, unit), :] = high
                    rhat[j, c, pl.ds(first + r * rows + low_at, unit), :] = low
        return carry

    lax.fori_loop(0, rows // unit, refs_tile, 0)
    quad_ref[...] = (0.5 * LOG2E) * lax.dot_general(
        power, shell_w, (((1,), (1,)), ((), ())), precision=EXACT, preferred_element_type=f32
    )

    def both_halves(ref, j):
        return jnp.concatenate([ref[j, 0], ref[j, 1]], axis=1)

    def cross_step(j, high_ref, low_ref, out):
        left = both_halves(rhat, j)
        wide = lax.dot_general(
            left, both_halves(high_ref, j), (((1,), (1,)), ((), ())), preferred_element_type=f32
        )
        rest = lax.dot_general(
            left[: 2 * rows],
            both_halves(low_ref, j),
            (((1,), (1,)), ((), ())),
            preferred_element_type=f32,
        )
        out[j, :, : wide.shape[1]] = wide[: 2 * rows] + wide[2 * rows :] + rest

    steps = PAIRS // (TILES - tiles_a)

    def late_tile(index, carry):
        for step in range(steps):
            cross_step(index * steps + step, fhi, flo, xs)
        feature_tile(tiles_a + index, fhi_b, flo_b, tiles_a)
        return carry

    lax.fori_loop(0, TILES - tiles_a, late_tile, 0)

    row_tiles = rows // 8
    lane = lax.broadcasted_iota(jnp.int32, (8, LANES), 1)
    packed_lanes = row_tiles * count_img
    spots = [(r // 2, r % 2) for r in range(ROT)]

    def load_unit(ref, k, t, j, part):
        return ref[j, pl.ds(k + part * rows, 8), t * LANES : (t + 1) * LANES]

    def score_unit(pairs, put, carry):
        top, total = carry
        values = idft36(pairs)
        for r, value in enumerate(values):
            put(*spots[r], value)
        best = jnp.maximum(top, tree(jnp.maximum, values))
        total = total * jnp.exp2(top - best)
        return best, total + tree(jnp.add, [jnp.exp2(value - best) for value in values])

    def score_tile(ref, k, t, carry):
        pairs = [tuple(load_unit(ref, k, t, j, part) for part in range(2)) for j in range(PAIRS)]
        pairs[0] = (pairs[0][0] - quad_ref[pl.ds(k, 8), :], pairs[0][1])

        def put(j, part, value):
            ref[j, pl.ds(k + part * rows, 8), t * LANES : (t + 1) * LANES] = value

        return score_unit(pairs, put, carry)

    steps_b = PAIRS // row_tiles

    def mixed_tile(index, carry):
        for step in range(steps_b):
            cross_step(index * steps_b + step, fhi_b, flo_b, xs_b)
        k = pl.multiple_of(index * 8, 8)
        return tuple(score_tile(xs, k, t, carry[t]) for t in range(2))

    carry = (jnp.full((8, LANES), -BIG, f32), jnp.zeros((8, LANES), f32))
    carry = lax.fori_loop(0, row_tiles, mixed_tile, (carry, carry))

    def score_pair(index, carry):
        k = pl.multiple_of(index * 16, 16)
        return tuple(score_tile(xs_b, k + 8 * i, 0, carry[i]) for i in range(2))

    carry, other = lax.fori_loop(0, row_tiles // 2, score_pair, carry)
    best = jnp.maximum(carry[0], other[0])
    carry = (
        best,
        carry[1] * jnp.exp2(carry[0] - best) + other[1] * jnp.exp2(other[0] - best),
    )

    def side_by_side(load):
        value = load(0)
        for k in range(1, row_tiles):
            value = jnp.where(
                lane < k * count_img, value, pltpu.roll(load(k), k * count_img, 1)
            )
        return value

    pairs = [
        tuple(side_by_side(lambda k: load_unit(xs_b, k * 8, 1, j, part)) for part in range(2))
        for j in range(PAIRS)
    ]
    shared = side_by_side(lambda k: quad_ref[k * 8 : (k + 1) * 8, :])
    pairs[0] = (jnp.where(lane < packed_lanes, pairs[0][0] - shared, -BIG), pairs[0][1])

    def put_packed(j, part, value):
        xp[j, part * 8 : (part + 1) * 8, :] = value

    best, total = score_unit(pairs, put_packed, carry)

    def fold(value, combine):
        reach = count_img
        while reach < LANES:
            value = combine(value, pltpu.roll(value, reach, 1))
            reach *= 2
        return jnp.concatenate([value] * 8, axis=0)

    top = fold(jnp.max(best, axis=0, keepdims=True), jnp.maximum)
    norm = fold(jnp.sum(total * jnp.exp2(best - top), axis=0, keepdims=True), jnp.add)
    scale = 1.0 / norm
    scale_row = jnp.concatenate([scale[:1], scale[:1]], axis=1)
    sums[0] = top

    def exp_unit(get, put):
        high = sums[0]
        scores = [get(*spot) for spot in spots]
        for j, pair in enumerate(dft36(lambda q: jnp.exp2(scores[q] - high))):
            for part, value in enumerate(pair):
                put(j, part, value)

    def exp_tile(ref, k, t):
        def put(j, part, value):
            ref[j, pl.ds(k + part * rows, 8), t * LANES : (t + 1) * LANES] = value

        exp_unit(lambda j, part: load_unit(ref, k, t, j, part), put)

    def exp_pair(index, carry):
        k = pl.multiple_of(index * 8, 8)
        for t in range(2):
            exp_tile(xs, k, t)
        return carry

    lax.fori_loop(0, row_tiles, exp_pair, 0)

    def products(j, ref, high_ref):
        count = high_ref.shape[2]
        left = (ref[j][:, :count] * scale_row[:, :count]).astype(bf16)
        return jnp.dot(left, both_halves(high_ref, j), preferred_element_type=f32)

    def back_first(index, carry):
        for step in range(steps_b):
            j = index * steps_b + step
            part_sums[j] = products(j, xs, fhi)
        exp_tile(xs_b, pl.multiple_of(index * 8, 8), 0)
        return carry

    lax.fori_loop(0, row_tiles, back_first, 0)
    exp_unit(
        lambda j, part: xp[j, part * 8 : (part + 1) * 8, :],
        put_packed,
    )
    for j in range(PAIRS):
        for part in range(2):
            value = xp[j, part * 8 : (part + 1) * 8, :]
            for k in range(row_tiles):
                at = slice(part * rows + k * 8, part * rows + (k + 1) * 8)
                xs_b[j, at, LANES:] = (
                    pltpu.roll(value, LANES - k * count_img, 1) if k else value
                )

    occupancy = []
    for k in range(row_tiles):
        at = slice(k * 8, (k + 1) * 8)
        rest = jnp.where(lane < count_img, xs_b[0, at, LANES:], 0.0)
        occupancy.append(
            (xs[0, at, :LANES] + xs[0, at, LANES:] + xs_b[0, at, :LANES] + rest) * scale
        )
    field = jnp.dot(
        jnp.concatenate(occupancy, axis=0), shell_w, precision=EXACT, preferred_element_type=f32
    )
    high = field.astype(bf16).astype(f32)
    first_lane = lax.rem(lax.broadcasted_iota(jnp.int32, (rows, SPAN), 1), STEP) == 0
    field = jnp.where(first_lane, high, field - high)

    for j in range(PAIRS):
        value = part_sums[j] + products(j, xs_b, fhi_b)
        if j:
            numh[j, :rows] = value[:rows, :SPAN] + value[rows:, SPAN:]
            numh[j, rows:] = value[:rows, SPAN:] - value[rows:, :SPAN]
        else:
            numh[j, :rows] = 0.5 * value[:rows, :SPAN]
            numh[j, rows:] = 0.5 * value[rows:, SPAN:]

    def number_tile(tile, carry):
        k = pl.multiple_of(tile * 8, 8)
        pairs = [
            tuple(numh[j, pl.ds(k + part * rows, 8), :] for part in range(2)) for j in range(PAIRS)
        ]
        for q, value in enumerate(idft36(pairs)):
            h, start = row_of(q)
            flat[h, pl.ds(start + k, 8), :] = value
        return carry

    lax.fori_loop(0, row_tiles, number_tile, 0)
    for h in range(halves):
        flat[h, width : width + rows, :] = field
        if padded > width + rows:
            flat[h, width + rows :, :] = jnp.zeros((padded - width - rows, SPAN), f32)
        for b in range(padded // LANES):
            block = flat[h, b * LANES : (b + 1) * LANES, :].T
            for g in range(SPAN // group_rows):
                cols_t[h, g, :, b * LANES : (b + 1) * LANES] = block[
                    g * group_rows : (g + 1) * group_rows
                ]

    def block_for(device):
        return cols_t[lax.rem(device, halves), lax.div(device, halves)]

    pairs = []
    for offset in [*range(1, half), 0]:
        slot = ahead(offset)
        pay[offset] = block_for(2 * slot + 1 - core).astype(bf16)
        copy = remote(
            pay.at[offset], mid.at[offset], pair_send.at[offset], pair_recv.at[offset], partner
        )
        copy.start()
        pairs.append(copy)

    lasts = []
    for index, offset in enumerate([*range(1, half), 0]):
        own = block_for(2 * ahead(offset) + core)
        pairs[index].wait_recv()
        value = own + mid[offset].astype(f32)
        if offset:
            mixed[offset] = value.astype(bf16)
            copy = remote(
                mixed.at[offset],
                final.at[offset],
                last_send.at[offset],
                last_recv.at[offset],
                2 * ahead(offset) + core,
            )
            copy.start()
            lasts.append(copy)
        else:
            result = value
    for index, copy in enumerate(lasts):
        copy.wait_recv()
        result = result + final[index + 1].astype(f32)
    weights = result[:, width : width + rows]
    for i in range(pieces):
        inverse = weights[i * STEP : i * STEP + 1] + weights[i * STEP + 1 : i * STEP + 2] + 1.0
        inverse = (2.0 / ROT) / inverse
        for q in range(turns):
            fin[i * piece + q * STEP : i * piece + (q + 1) * STEP, :] = (
                result[i * STEP : (i + 1) * STEP, q * rows : (q + 1) * rows] * inverse
            )
    out_ref[...] = fin[...].T
    for copy in far + near + pairs + lasts:
        copy.wait_send()


def on_device(images, class_refs, sigma2, ctf_group, defocus_bin):
    count_dev = lax.axis_size("img")
    half = count_dev // 2
    count_img = images.shape[0]
    share = class_refs.shape[1]
    piece, halves, pieces, turns, width, padded = geometry(share)
    group_rows = STEP * pieces
    count_n = (SHIFTS + 1) * count_img
    count_a = 2 * LANES
    count_b = count_n - count_a
    travel = pltpu.VMEM((half, group_rows, padded), jnp.bfloat16)
    return pl.pallas_call(
        lambda *refs: em_kernel(count_dev, *refs),
        out_shape=jax.ShapeDtypeStruct(class_refs.shape, jnp.float32),
        in_specs=[pl.BlockSpec(memory_space=pltpu.VMEM)] * 7,
        out_specs=pl.BlockSpec(memory_space=pltpu.VMEM),
        scratch_shapes=[
            pltpu.VMEM((SLOTS, 2, ROT * count_img, SPAN), jnp.float32),
            pltpu.VMEM((PAIRS, 2, count_a, SPAN), jnp.bfloat16),
            pltpu.VMEM((PAIRS, 2, count_a, SPAN), jnp.bfloat16),
            pltpu.VMEM((PAIRS, 2, count_b, SPAN), jnp.bfloat16),
            pltpu.VMEM((PAIRS, 2, count_b, SPAN), jnp.bfloat16),
            pltpu.VMEM((PAIRS, 2, 4 * CLASSES, SPAN), jnp.bfloat16),
            pltpu.VMEM((PAIRS, 2 * CLASSES, 2 * LANES), jnp.float32),
            pltpu.VMEM((PAIRS, 2 * CLASSES, 2 * LANES), jnp.float32),
            pltpu.VMEM((PAIRS, 16, LANES), jnp.float32),
            pltpu.VMEM((CLASSES, LANES), jnp.float32),
            pltpu.VMEM((1, 8, LANES), jnp.float32),
            pltpu.VMEM((PAIRS, 2 * CLASSES, 2 * SPAN), jnp.float32),
            pltpu.VMEM((PAIRS, 2 * CLASSES, SPAN), jnp.float32),
            pltpu.VMEM((halves, padded, SPAN), jnp.float32),
            pltpu.VMEM((halves, SPAN // group_rows, group_rows, padded), jnp.float32),
            pltpu.VMEM((share, CLASSES), jnp.float32),
            pltpu.VMEM((group_rows, padded), jnp.bfloat16),
            pltpu.VMEM((count_dev, group_rows, padded), jnp.bfloat16),
            travel,
            travel,
            travel,
            travel,
        ]
        + [pltpu.SemaphoreType.DMA((half,))] * 8,
        compiler_params=pltpu.CompilerParams(
            vmem_limit_bytes=60 * 2**20, collective_id=0, has_side_effects=True
        ),
        name="em_step",
    )(
        images,
        class_refs,
        sigma2,
        ctf_group.reshape(1, count_img),
        defocus_bin.reshape(1, count_img),
        jnp.asarray(ctf_lanes()),
        jnp.asarray(phase_parts()),
    )


def solution(mesh):
    in_specs = (
        P(("groups", "img"), None),
        P("groups", "img"),
        P("groups", None),
        P(("groups", "img")),
        P(("groups", "img")),
    )
    out_specs = P("groups", "img")
    return jax.shard_map(
        on_device, mesh=mesh, in_specs=in_specs, out_specs=out_specs, check_vma=False
    )
```

```python
import math

import jax
import jax.numpy as jnp
import numpy as np
from jax import lax
from jax.experimental import pallas as pl
from jax.experimental.pallas import tpu as pltpu
from jax.sharding import PartitionSpec as P

CLASSES = 48
ROT = 36
SHELLS = 16
ANG = 144
REACH = 3
SHIFTS = 49
BINS = 32
NGROUP = 16

LANES = 128
PARTS = 2 * SHELLS
STEP = ANG // ROT
SPAN = STEP * PARTS
WIDTH = ROT * SPAN
SIDE = 2 * REACH + 1
PAIRS = ROT // 2
TILES = (SHIFTS + 1) // 2
SLOTS = SIDE + 2
BIG = 1e30
LOG2E = math.log2(math.e)
EXACT = lax.Precision.HIGHEST


def phase_parts():
    angles = 2.0 * np.pi * np.arange(ANG) / ANG
    radius = (np.arange(SHELLS) + 1.0) / (2.0 * SHELLS)
    tables = []
    for direction in (np.sin(angles), np.cos(angles)):
        for offset in range(1, REACH + 1):
            phase = 2.0 * np.pi * offset * direction[None, :] * radius[:, None]
            both = []
            for cosine, sine in ((np.cos(phase), -np.sin(phase)), (np.cos(phase), np.sin(phase))):
                both.append(np.stack([cosine, sine]))
            table = np.stack(both, axis=1)
            table = table.reshape(2, PARTS, ROT, STEP).transpose(0, 2, 1, 3)
            tables.append(table.reshape(2, ROT, SPAN))
    tables.append(np.ones((2, ROT, SPAN)))
    return np.stack(tables).astype(np.float32)


def ctf_lanes():
    radius = (np.arange(SHELLS) + 1.0) / (2.0 * SHELLS)
    defocus = 1.0 + np.arange(BINS) / BINS
    table = -np.sin(80.0 * defocus[:, None] * radius**2 + 0.1)
    return np.tile(np.repeat(table, STEP, axis=1), (1, 2)).astype(np.float32)


COS9 = [math.cos(2.0 * math.pi * k / 9.0) for k in range(5)]
SIN9 = [math.sin(2.0 * math.pi * k / 9.0) for k in range(5)]


def even9(first, s1, s2, s3, s4):
    c1, c2 = COS9[1], COS9[2]
    a, b = s1 - s4, s2 - s4
    g1 = c1 * a + c2 * b
    g2 = c2 * (a - b) - c1 * b
    t = s1 + s2 + s4
    w = first + s3
    u = first - 0.5 * s3
    return [w + t, u + g1, u + g2, w - 0.5 * t, u - (g1 + g2)]


def odd9(d1, d2, d3, d4):
    n1, n3, n4 = SIN9[1], SIN9[3], SIN9[4]
    a, b, c = d1 + d2, d2 + d4, d1 - d4
    h1 = n1 * a + n4 * b
    h2 = n1 * c + n4 * a
    e = n3 * d3
    return [h1 + e, h2 - e, n3 * (d1 - d2 + d4), h2 - h1 + e]


def where_q(a, b):
    return (9 * a + 4 * b) % ROT


def dft36(load):
    parts = []
    for a in range(4):
        x = [load(where_q(a, b)) for b in range(9)]
        s = [x[j] + x[9 - j] for j in range(1, 5)]
        d = [x[9 - j] - x[j] for j in range(1, 5)]
        parts.append((even9(x[0], *s), [None] + odd9(*d)))
    y = [part[0][0] for part in parts]
    p, m = y[0] + y[2], y[1] + y[3]
    pairs = [(p + m, p - m), (y[0] - y[2], y[3] - y[1])]
    for g in range(1, 5):
        re = [part[0][g] for part in parts]
        im = [part[1][g] for part in parts]
        rp, rm, ip, im_ = re[0] + re[2], re[0] - re[2], im[0] + im[2], im[0] - im[2]
        sp, sm, jp, jm = re[1] + re[3], re[1] - re[3], im[1] + im[3], im[1] - im[3]
        pairs.append((rp + sp, ip + jp))
        pairs.append((rm + jm, im_ - sm))
        pairs.append((rp - sp, ip - jp))
        pairs.append((rm - jm, im_ + sm))
    return pairs


def idft36(pairs):
    p, m = pairs[0][0] + pairs[0][1], pairs[0][0] - pairs[0][1]
    re, im = pairs[1]
    parts = [[(p + re, None)], [(m - im, None)], [(p - re, None)], [(m + im, None)]]
    for g in range(4):
        (r0, i0), (r1, i1), (r2, i2), (r3, i3) = pairs[2 + 4 * g : 6 + 4 * g]
        rp, rm, ip, im_ = r0 + r2, r0 - r2, i0 + i2, i0 - i2
        sp, sm, jp, jm = r1 + r3, r1 - r3, i1 + i3, i1 - i3
        parts[0].append((rp + sp, ip + jp))
        parts[1].append((rm - jm, im_ + sm))
        parts[2].append((rp - sp, ip - jp))
        parts[3].append((rm + jm, im_ - sm))
    out = [None] * ROT
    for a in range(4):
        y = parts[a]
        even = even9(y[0][0], y[1][0], y[2][0], y[3][0], y[4][0])
        odd = [None] + odd9(y[1][1], y[2][1], y[3][1], y[4][1])
        out[where_q(a, 0)] = even[0]
        for b in range(1, 5):
            out[where_q(a, b)] = even[b] - odd[b]
            out[where_q(a, 9 - b)] = even[b] + odd[b]
    return out


def split(value):
    high = value.astype(jnp.bfloat16)
    return high, (value - high.astype(jnp.float32)).astype(jnp.bfloat16)


def image_blocks(img_ref):
    count = img_ref.shape[0]
    lane = lax.broadcasted_iota(jnp.int32, (count, LANES), 1)
    source = [
        img_ref[:, v * LANES : (v + 1) * LANES].astype(jnp.float32)
        for v in range(img_ref.shape[1] // LANES)
    ]
    per = LANES // STEP
    rows = []
    for p in range(PARTS):
        v, shift = divmod(p * ANG, LANES)
        value = source[v]
        if shift:
            value = jnp.where(
                lane < LANES - shift,
                pltpu.roll(source[v], LANES - shift, 1),
                pltpu.roll(source[v + 1], LANES - shift, 1),
            )
        rows.append(value)
    reach = 1
    while reach < per:
        low = (lane & (reach * STEP)) == 0
        new = list(rows)
        for p in range(per):
            if not p & reach:
                first, second = rows[p], rows[p + reach]
                new[p] = jnp.where(low, first, pltpu.roll(second, reach * STEP, 1))
                new[p + reach] = jnp.where(
                    low, pltpu.roll(first, LANES - reach * STEP, 1), second
                )
        rows = new
        reach *= 2
    for q in range(per, ROT):
        value = None
        for p in range(PARTS):
            v, start = divmod(p * ANG + q * STEP, LANES)
            moved = pltpu.roll(source[v], (p * STEP - start) % LANES, 1)
            if value is None:
                value = moved
            else:
                value = jnp.where(lane < p * STEP, value, moved)
        rows.append(value)
    return rows


def tree(combine, values):
    while len(values) > 1:
        joined = [combine(a, b) for a, b in zip(values[::2], values[1::2])]
        values = joined + values[len(joined) * 2 :]
    return values[0]


def geometry(share):
    piece = min(share, ANG)
    halves = ANG // piece
    pieces = share // piece
    turns = piece // STEP
    width = turns * CLASSES
    padded = -(-(width + CLASSES) // LANES) * LANES
    return piece, halves, pieces, turns, width, padded


def em_kernel(
    count_dev,
    img_hbm,
    refs_hbm,
    sigma_hbm,
    group_hbm,
    bin_hbm,
    ctf_hbm,
    phase_hbm,
    out_ref,
    img_ref,
    refs_ref,
    sigma_ref,
    group_ref,
    bin_ref,
    ctf_ref,
    phase_ref,
    moved,
    fhi,
    flo,
    rhat,
    xs,
    xs_b,
    xp,
    quad_ref,
    sums,
    numh,
    flat,
    cols_t,
    fin,
    mine,
    got,
    pay,
    mid,
    mixed,
    final,
    near_send,
    near_recv,
    far_send,
    far_recv,
    pair_send,
    pair_recv,
    last_send,
    last_recv,
    load_sem,
):
    rows = CLASSES
    count_img = img_ref.shape[0]
    share = refs_ref.shape[1]
    piece, halves, pieces, turns, width, padded = geometry(share)
    group_rows = STEP * pieces
    count_n = fhi.shape[2]
    count_a = 2 * LANES
    half = count_dev // 2
    me = lax.axis_index("img")
    core = lax.rem(me, 2)
    place = lax.div(me, 2)
    partner = me + 1 - 2 * core
    f32, bf16 = jnp.float32, jnp.bfloat16

    def ahead(offset):
        return lax.rem(place + offset, half)

    def behind(offset):
        return lax.rem(place + half - offset, half)

    barrier = pltpu.get_barrier_semaphore()
    for offset in range(1, half):
        pl.semaphore_signal(
            barrier,
            inc=1,
            device_id={"img": 2 * ahead(offset) + core},
            device_id_type=pl.DeviceIdType.MESH,
        )
    pl.semaphore_signal(
        barrier, inc=1, device_id={"img": partner}, device_id_type=pl.DeviceIdType.MESH
    )

    def remote(source, target, send, recv, device):
        return pltpu.make_async_remote_copy(
            src_ref=source,
            dst_ref=target,
            send_sem=send,
            recv_sem=recv,
            device_id={"img": device},
            device_id_type=pl.DeviceIdType.MESH,
        )

    loads = [
        pltpu.make_async_copy(source, target, load_sem.at[index])
        for index, (source, target) in enumerate(
            (
                (refs_hbm, refs_ref),
                (img_hbm, img_ref),
                (sigma_hbm, sigma_ref),
                (group_hbm, group_ref),
                (bin_hbm, bin_ref),
                (ctf_hbm, ctf_ref),
                (phase_hbm, phase_ref),
            )
        )
    ]
    for copy in loads:
        copy.start()
    loads[0].wait()

    fin[...] = refs_ref[...].astype(f32).T
    turned = []
    for q in range(turns):
        turned.append(
            jnp.concatenate(
                [fin[i * piece + q * STEP : i * piece + (q + 1) * STEP, :] for i in range(pieces)],
                axis=0,
            )
        )
    turned.append(jnp.zeros((group_rows, padded - width), f32))
    own = jnp.concatenate(turned, axis=1).astype(bf16)
    mine[...] = own
    got[me] = own
    pl.semaphore_wait(barrier, half)

    far = [
        remote(
            mine,
            got.at[me],
            far_send.at[offset],
            far_recv.at[offset],
            2 * ahead(offset) + core,
        )
        for offset in range(1, half)
    ]
    near = [remote(mine, got.at[me], near_send.at[0], near_recv.at[0], partner)]
    for copy in far + near:
        copy.start()

    for copy in loads[1:]:
        copy.wait()

    blocks = image_blocks(img_ref)

    def pick(ids, table):
        hot = ids == lax.broadcasted_iota(jnp.int32, (table.shape[0], count_img), 0)
        return lax.dot_general(
            hot.astype(f32),
            table,
            (((0,), (0,)), ((), ())),
            precision=EXACT,
            preferred_element_type=f32,
        )

    lane_shell = lax.rem(
        lax.div(lax.broadcasted_iota(jnp.int32, (SHELLS, SPAN), 1), STEP), SHELLS
    )
    spread = (lane_shell == lax.broadcasted_iota(jnp.int32, (SHELLS, SPAN), 0)).astype(f32)
    noise = jnp.dot(
        pick(group_ref[...], sigma_ref[...]), spread, precision=EXACT, preferred_element_type=f32
    )
    ctf = pick(bin_ref[...], ctf_ref[...])
    weight = ctf / noise
    shell_w = jnp.concatenate([ctf * ctf / noise] * (LANES // count_img), axis=0)

    for q in range(ROT):
        at = slice(q * count_img, (q + 1) * count_img)
        value = blocks[q] * weight
        other = pltpu.roll(value, SPAN // 2, 1)
        for slot in (REACH, SIDE):
            moved[slot, 0, at, :] = value
            moved[slot, 1, at, :] = other
        moved[SIDE + 1, 0, at, :] = 0.5 * value
        moved[SIDE + 1, 1, at, :] = 0.5 * value
        for offset in range(1, REACH + 1):
            c = phase_ref[REACH + offset - 1, 0, q : q + 1, :]
            s = phase_ref[REACH + offset - 1, 1, q : q + 1, :]
            vc, os, oc, vs = value * c, other * s, other * c, value * s
            moved[REACH + offset, 0, at, :] = vc + os
            moved[REACH + offset, 1, at, :] = oc - vs
            moved[REACH - offset, 0, at, :] = vc - os
            moved[REACH - offset, 1, at, :] = oc + vs

    both = 2 * count_img

    def feature_tile(tile, carry):
        slot = lax.div(tile, REACH)
        entry = lax.rem(tile, REACH) + REACH * (lax.div(tile, REACH * SIDE)) + REACH * lax.div(
            tile, TILES - 1
        )
        start = pl.multiple_of(tile * both, both)

        def load(q):
            at = slice(q * count_img, (q + 1) * count_img)
            a = moved[slot, 0, at, :] * phase_ref[entry, 0, q : q + 1, :]
            b = moved[slot, 1, at, :] * phase_ref[entry, 1, q : q + 1, :]
            return jnp.concatenate([a + b, a - b], axis=0).astype(bf16).astype(f32)

        for j, pair in enumerate(dft36(load)):
            for part, value in enumerate(pair):
                high, low = split(value)
                fhi[j, part, pl.ds(start, both), :] = high
                flo[j, part, pl.ds(start, both), :] = low
        return carry

    def relay(offset):
        source = 2 * behind(offset) + core
        return remote(
            got.at[source], got.at[source], near_send.at[offset], near_recv.at[offset], partner
        )

    def relay_step(index, carry):
        offset = index + 1
        source = 2 * behind(offset) + core
        remote(
            mine, got.at[source], far_send.at[offset], far_recv.at[offset], partner
        ).wait_recv()
        relay(offset).start()
        first = early + index * per_relay
        lax.fori_loop(first, first + per_relay, feature_tile, 0)
        return carry

    per_relay = max(1, TILES // (2 * (half - 1)) + 1) if half - 1 <= TILES // 2 else 1
    relayed = min(half - 1, TILES // per_relay)
    early = TILES - relayed * per_relay
    lax.fori_loop(0, early, feature_tile, 0)
    lax.fori_loop(0, relayed, relay_step, 0)
    for offset in range(relayed + 1, half):
        far[offset - 1].wait_recv()
        relay(offset).start()
    near += [relay(offset) for offset in range(1, half)]
    for j in range(PAIRS):
        xs_b[j, :, LANES:] = jnp.zeros((2 * rows, LANES), f32)
    for offset in range(half):
        near[offset].wait_recv()

    for h in range(halves):
        for b in range(padded // LANES):
            block = jnp.concatenate(
                [
                    got[g * halves + h][:, b * LANES : (b + 1) * LANES].astype(f32)
                    for g in range(SPAN // group_rows)
                ],
                axis=0,
            )
            flat[h, b * LANES : (b + 1) * LANES, :] = block.T

    def row_of(q):
        return q // turns, (q % turns) * rows

    power = jnp.zeros((rows, SPAN), f32)
    for q in range(ROT):
        h, start = row_of(q)
        block = flat[h, start : start + rows, :]
        power = power + block * block
    unit = 16

    def refs_tile(tile, carry):
        first = pl.multiple_of(tile * unit, unit)

        def load(q):
            h, start = row_of(q)
            return flat[h, pl.ds(start + first, unit), :]

        low_at = 2 * rows
        for j, (re, im) in enumerate(dft36(load)):
            scale = LOG2E / ROT if j == 0 else 2.0 * LOG2E / ROT
            re, im = scale * re, scale * im
            grid = [[re, im], [-im, re]]
            if j == 0:
                zero = jnp.zeros_like(re)
                grid = [[re, zero], [zero, im]]
            for r in range(2):
                for c in range(2):
                    high, low = split(grid[r][c])
                    rhat[j, c, pl.ds(first + r * rows, unit), :] = high
                    rhat[j, c, pl.ds(first + r * rows + low_at, unit), :] = low
        return carry

    lax.fori_loop(0, rows // unit, refs_tile, 0)
    quad_ref[...] = (0.5 * LOG2E) * lax.dot_general(
        power, shell_w, (((1,), (1,)), ((), ())), precision=EXACT, preferred_element_type=f32
    )

    def both_halves(ref, j):
        return jnp.concatenate([ref[j, 0], ref[j, 1]], axis=1)

    for j in range(PAIRS):
        left = both_halves(rhat, j)
        wide = lax.dot_general(
            left, both_halves(fhi, j), (((1,), (1,)), ((), ())), preferred_element_type=f32
        )
        rest = lax.dot_general(
            left[: 2 * rows],
            both_halves(flo, j),
            (((1,), (1,)), ((), ())),
            preferred_element_type=f32,
        )
        value = wide[: 2 * rows] + wide[2 * rows :] + rest
        xs[j] = value[:, :count_a]
        xs_b[j, :, : count_n - count_a] = value[:, count_a:]

    row_tiles = rows // 8
    lane = lax.broadcasted_iota(jnp.int32, (8, LANES), 1)
    packed_lanes = row_tiles * count_img
    spots = [(r // 2, r % 2) for r in range(ROT)]

    def load_unit(ref, k, t, j, part):
        return ref[j, pl.ds(k + part * rows, 8), t * LANES : (t + 1) * LANES]

    def score_unit(pairs, put, best):
        values = idft36(pairs)
        for r, value in enumerate(values):
            put(*spots[r], value)
        return jnp.maximum(best, tree(jnp.maximum, values))

    def score_tile(ref, k, t, carry):
        pairs = [tuple(load_unit(ref, k, t, j, part) for part in range(2)) for j in range(PAIRS)]
        pairs[0] = (pairs[0][0] - quad_ref[pl.ds(k, 8), :], pairs[0][1])

        def put(j, part, value):
            ref[j, pl.ds(k + part * rows, 8), t * LANES : (t + 1) * LANES] = value

        return score_unit(pairs, put, carry)

    def score_pair(index, best):
        k = pl.multiple_of(index * 8, 8)
        return tuple(score_tile(xs, k, t, best[t]) for t in range(2))

    def score_pair_b(index, best):
        k = pl.multiple_of(index * 16, 16)
        return tuple(score_tile(xs_b, k + 8 * i, 0, best[i]) for i in range(2))

    best = jnp.full((8, LANES), -BIG, f32)
    best = lax.fori_loop(0, row_tiles, score_pair, (best, best))
    best = lax.fori_loop(0, row_tiles // 2, score_pair_b, best)
    best = jnp.maximum(*best)

    def side_by_side(load):
        value = load(0)
        for k in range(1, row_tiles):
            value = jnp.where(
                lane < k * count_img, value, pltpu.roll(load(k), k * count_img, 1)
            )
        return value

    pairs = [
        tuple(side_by_side(lambda k: load_unit(xs_b, k * 8, 1, j, part)) for part in range(2))
        for j in range(PAIRS)
    ]
    shared = side_by_side(lambda k: quad_ref[k * 8 : (k + 1) * 8, :])
    pairs[0] = (jnp.where(lane < packed_lanes, pairs[0][0] - shared, -BIG), pairs[0][1])

    def put_packed(j, part, value):
        xp[j, part * 8 : (part + 1) * 8, :] = value

    best = score_unit(pairs, put_packed, best)

    def fold(value, combine):
        reach = count_img
        while reach < LANES:
            value = combine(value, pltpu.roll(value, reach, 1))
            reach *= 2
        return jnp.concatenate([value] * 8, axis=0)

    top = fold(jnp.max(best, axis=0, keepdims=True), jnp.maximum)
    sums[0] = top

    def exp_unit(get, put):
        high = sums[0]
        scores = [get(*spot) for spot in spots]
        pairs = dft36(lambda q: jnp.exp2(scores[q] - high))
        for j, pair in enumerate(pairs):
            for part, value in enumerate(pair):
                put(j, part, value)
        return pairs[0][0]

    def exp_tile(ref, k, t):
        def put(j, part, value):
            ref[j, pl.ds(k + part * rows, 8), t * LANES : (t + 1) * LANES] = value

        return exp_unit(lambda j, part: load_unit(ref, k, t, j, part), put)

    def exp_pair(index, total):
        k = pl.multiple_of(index * 8, 8)
        return total + exp_tile(xs, k, 0) + exp_tile(xs, k, 1)

    def exp_pair_b(index, total):
        k = pl.multiple_of(index * 16, 16)
        return total + exp_tile(xs_b, k, 0) + exp_tile(xs_b, k + 8, 0)

    total = exp_unit(lambda j, part: xp[j, part * 8 : (part + 1) * 8, :], put_packed)
    total = lax.fori_loop(0, row_tiles, exp_pair, total)
    total = lax.fori_loop(0, row_tiles // 2, exp_pair_b, total)
    norm = fold(jnp.sum(total, axis=0, keepdims=True), jnp.add)
    scale = 1.0 / norm
    scale_row = jnp.concatenate([scale[:1]] * 4, axis=1)
    for j in range(PAIRS):
        for part in range(2):
            value = xp[j, part * 8 : (part + 1) * 8, :]
            for k in range(row_tiles):
                at = slice(part * rows + k * 8, part * rows + (k + 1) * 8)
                xs_b[j, at, LANES:] = (
                    pltpu.roll(value, LANES - k * count_img, 1) if k else value
                )

    occupancy = []
    for k in range(row_tiles):
        at = slice(k * 8, (k + 1) * 8)
        rest = jnp.where(lane < count_img, xs_b[0, at, LANES:], 0.0)
        occupancy.append(
            (xs[0, at, :LANES] + xs[0, at, LANES:] + xs_b[0, at, :LANES] + rest) * scale
        )
    field = jnp.dot(
        jnp.concatenate(occupancy, axis=0), shell_w, precision=EXACT, preferred_element_type=f32
    )
    high = field.astype(bf16).astype(f32)
    first_lane = lax.rem(lax.broadcasted_iota(jnp.int32, (rows, SPAN), 1), STEP) == 0
    field = jnp.where(first_lane, high, field - high)

    for j in range(PAIRS):
        left = jnp.concatenate([xs[j], xs_b[j]], axis=1)
        left = (left * scale_row).astype(bf16)[:, :count_n]
        value = jnp.dot(left, both_halves(fhi, j), preferred_element_type=f32)
        if j:
            numh[j, :rows] = value[:rows, :SPAN] + value[rows:, SPAN:]
            numh[j, rows:] = value[:rows, SPAN:] - value[rows:, :SPAN]
        else:
            numh[j, :rows] = 0.5 * value[:rows, :SPAN]
            numh[j, rows:] = 0.5 * value[rows:, SPAN:]

    def number_tile(tile, carry):
        k = pl.multiple_of(tile * 8, 8)
        pairs = [
            tuple(numh[j, pl.ds(k + part * rows, 8), :] for part in range(2)) for j in range(PAIRS)
        ]
        for q, value in enumerate(idft36(pairs)):
            h, start = row_of(q)
            flat[h, pl.ds(start + k, 8), :] = value
        return carry

    lax.fori_loop(0, row_tiles, number_tile, 0)
    for h in range(halves):
        flat[h, width : width + rows, :] = field
        if padded > width + rows:
            flat[h, width + rows :, :] = jnp.zeros((padded - width - rows, SPAN), f32)
        for b in range(padded // LANES):
            block = flat[h, b * LANES : (b + 1) * LANES, :].T
            for g in range(SPAN // group_rows):
                cols_t[h, g, :, b * LANES : (b + 1) * LANES] = block[
                    g * group_rows : (g + 1) * group_rows
                ]

    def block_for(device):
        return cols_t[lax.rem(device, halves), lax.div(device, halves)]

    pairs = []
    for offset in [*range(1, half), 0]:
        slot = ahead(offset)
        pay[offset] = block_for(2 * slot + 1 - core).astype(bf16)
        copy = remote(
            pay.at[offset], mid.at[offset], pair_send.at[offset], pair_recv.at[offset], partner
        )
        copy.start()
        pairs.append(copy)

    lasts = []
    for index, offset in enumerate([*range(1, half), 0]):
        own = block_for(2 * ahead(offset) + core)
        pairs[index].wait_recv()
        value = own + mid[offset].astype(f32)
        if offset:
            mixed[offset] = value.astype(bf16)
            copy = remote(
                mixed.at[offset],
                final.at[offset],
                last_send.at[offset],
                last_recv.at[offset],
                2 * ahead(offset) + core,
            )
            copy.start()
            lasts.append(copy)
        else:
            result = value
    for index, copy in enumerate(lasts):
        copy.wait_recv()
        result = result + final[index + 1].astype(f32)
    weights = result[:, width : width + rows]
    for i in range(pieces):
        inverse = weights[i * STEP : i * STEP + 1] + weights[i * STEP + 1 : i * STEP + 2] + 1.0
        inverse = (2.0 / ROT) / inverse
        for q in range(turns):
            fin[i * piece + q * STEP : i * piece + (q + 1) * STEP, :] = (
                result[i * STEP : (i + 1) * STEP, q * rows : (q + 1) * rows] * inverse
            )
    out_ref[...] = fin[...].T
    for copy in far + near + pairs + lasts:
        copy.wait_send()


def on_device(images, class_refs, sigma2, ctf_group, defocus_bin):
    count_dev = lax.axis_size("img")
    half = count_dev // 2
    count_img = images.shape[0]
    share = class_refs.shape[1]
    piece, halves, pieces, turns, width, padded = geometry(share)
    group_rows = STEP * pieces
    count_n = (SHIFTS + 1) * count_img
    travel = pltpu.VMEM((half, group_rows, padded), jnp.bfloat16)
    args = (
        images,
        class_refs,
        sigma2,
        ctf_group.reshape(1, count_img),
        defocus_bin.reshape(1, count_img),
        jnp.asarray(ctf_lanes()),
        jnp.asarray(phase_parts()),
    )
    return pl.pallas_call(
        lambda *refs: em_kernel(count_dev, *refs),
        out_shape=jax.ShapeDtypeStruct(class_refs.shape, jnp.float32),
        in_specs=[pl.BlockSpec(memory_space=pl.ANY)] * 7,
        out_specs=pl.BlockSpec(memory_space=pltpu.VMEM),
        scratch_shapes=[pltpu.VMEM(arg.shape, arg.dtype) for arg in args]
        + [
            pltpu.VMEM((SLOTS, 2, ROT * count_img, SPAN), jnp.float32),
            pltpu.VMEM((PAIRS, 2, count_n, SPAN), jnp.bfloat16),
            pltpu.VMEM((PAIRS, 2, count_n, SPAN), jnp.bfloat16),
            pltpu.VMEM((PAIRS, 2, 4 * CLASSES, SPAN), jnp.bfloat16),
            pltpu.VMEM((PAIRS, 2 * CLASSES, 2 * LANES), jnp.float32),
            pltpu.VMEM((PAIRS, 2 * CLASSES, 2 * LANES), jnp.float32),
            pltpu.VMEM((PAIRS, 16, LANES), jnp.float32),
            pltpu.VMEM((CLASSES, LANES), jnp.float32),
            pltpu.VMEM((1, 8, LANES), jnp.float32),
            pltpu.VMEM((PAIRS, 2 * CLASSES, SPAN), jnp.float32),
            pltpu.VMEM((halves, padded, SPAN), jnp.float32),
            pltpu.VMEM((halves, SPAN // group_rows, group_rows, padded), jnp.float32),
            pltpu.VMEM((share, CLASSES), jnp.float32),
            pltpu.VMEM((group_rows, padded), jnp.bfloat16),
            pltpu.VMEM((count_dev, group_rows, padded), jnp.bfloat16),
            travel,
            travel,
            travel,
            travel,
        ]
        + [pltpu.SemaphoreType.DMA((half,))] * 8
        + [pltpu.SemaphoreType.DMA((len(args),))],
        compiler_params=pltpu.CompilerParams(
            vmem_limit_bytes=60 * 2**20, collective_id=0, has_side_effects=True
        ),
        name="em_step",
    )(*args)


def solution(mesh):
    in_specs = (
        P(("groups", "img"), None),
        P("groups", "img"),
        P("groups", None),
        P(("groups", "img")),
        P(("groups", "img")),
    )
    out_specs = P("groups", "img")
    return jax.shard_map(
        on_device, mesh=mesh, in_specs=in_specs, out_specs=out_specs, check_vma=False
    )
```

```python
import math

import jax
import jax.numpy as jnp
import numpy as np
from jax import lax
from jax.experimental import pallas as pl
from jax.experimental.pallas import tpu as pltpu
from jax.sharding import PartitionSpec as P

CLASSES = 48
ROT = 36
SHELLS = 16
ANG = 144
REACH = 3
SHIFTS = 49
BINS = 32
NGROUP = 16

LANES = 128
PARTS = 2 * SHELLS
STEP = ANG // ROT
SPAN = STEP * PARTS
WIDTH = ROT * SPAN
SIDE = 2 * REACH + 1
PAIRS = ROT // 2
TILES = (SHIFTS + 1) // 2
SLOTS = SIDE + 2
BIG = 1e30
LOG2E = math.log2(math.e)
EXACT = lax.Precision.HIGHEST


def phase_parts():
    angles = 2.0 * np.pi * np.arange(ANG) / ANG
    radius = (np.arange(SHELLS) + 1.0) / (2.0 * SHELLS)
    tables = []
    for direction in (np.sin(angles), np.cos(angles)):
        for offset in range(1, REACH + 1):
            phase = 2.0 * np.pi * offset * direction[None, :] * radius[:, None]
            both = []
            for cosine, sine in ((np.cos(phase), -np.sin(phase)), (np.cos(phase), np.sin(phase))):
                both.append(np.stack([cosine, sine]))
            table = np.stack(both, axis=1)
            table = table.reshape(2, PARTS, ROT, STEP).transpose(0, 2, 1, 3)
            tables.append(table.reshape(2, ROT, SPAN))
    tables.append(np.ones((2, ROT, SPAN)))
    return np.stack(tables).astype(np.float32)


def ctf_lanes():
    radius = (np.arange(SHELLS) + 1.0) / (2.0 * SHELLS)
    defocus = 1.0 + np.arange(BINS) / BINS
    table = -np.sin(80.0 * defocus[:, None] * radius**2 + 0.1)
    return np.tile(np.repeat(table, STEP, axis=1), (1, 2)).astype(np.float32)


COS9 = [math.cos(2.0 * math.pi * k / 9.0) for k in range(5)]
SIN9 = [math.sin(2.0 * math.pi * k / 9.0) for k in range(5)]


def even9(first, s1, s2, s3, s4):
    c1, c2 = COS9[1], COS9[2]
    a, b = s1 - s4, s2 - s4
    g1 = c1 * a + c2 * b
    g2 = c2 * (a - b) - c1 * b
    t = s1 + s2 + s4
    w = first + s3
    u = first - 0.5 * s3
    return [w + t, u + g1, u + g2, w - 0.5 * t, u - (g1 + g2)]


def odd9(d1, d2, d3, d4):
    n1, n3, n4 = SIN9[1], SIN9[3], SIN9[4]
    a, b, c = d1 + d2, d2 + d4, d1 - d4
    h1 = n1 * a + n4 * b
    h2 = n1 * c + n4 * a
    e = n3 * d3
    return [h1 + e, h2 - e, n3 * (d1 - d2 + d4), h2 - h1 + e]


def where_q(a, b):
    return (9 * a + 4 * b) % ROT


def dft36(load):
    parts = []
    for a in range(4):
        x = [load(where_q(a, b)) for b in range(9)]
        s = [x[j] + x[9 - j] for j in range(1, 5)]
        d = [x[9 - j] - x[j] for j in range(1, 5)]
        parts.append((even9(x[0], *s), [None] + odd9(*d)))
    y = [part[0][0] for part in parts]
    p, m = y[0] + y[2], y[1] + y[3]
    pairs = [(p + m, p - m), (y[0] - y[2], y[3] - y[1])]
    for g in range(1, 5):
        re = [part[0][g] for part in parts]
        im = [part[1][g] for part in parts]
        rp, rm, ip, im_ = re[0] + re[2], re[0] - re[2], im[0] + im[2], im[0] - im[2]
        sp, sm, jp, jm = re[1] + re[3], re[1] - re[3], im[1] + im[3], im[1] - im[3]
        pairs.append((rp + sp, ip + jp))
        pairs.append((rm + jm, im_ - sm))
        pairs.append((rp - sp, ip - jp))
        pairs.append((rm - jm, im_ + sm))
    return pairs


def idft36(pairs):
    p, m = pairs[0][0] + pairs[0][1], pairs[0][0] - pairs[0][1]
    re, im = pairs[1]
    parts = [[(p + re, None)], [(m - im, None)], [(p - re, None)], [(m + im, None)]]
    for g in range(4):
        (r0, i0), (r1, i1), (r2, i2), (r3, i3) = pairs[2 + 4 * g : 6 + 4 * g]
        rp, rm, ip, im_ = r0 + r2, r0 - r2, i0 + i2, i0 - i2
        sp, sm, jp, jm = r1 + r3, r1 - r3, i1 + i3, i1 - i3
        parts[0].append((rp + sp, ip + jp))
        parts[1].append((rm - jm, im_ + sm))
        parts[2].append((rp - sp, ip - jp))
        parts[3].append((rm + jm, im_ - sm))
    out = [None] * ROT
    for a in range(4):
        y = parts[a]
        even = even9(y[0][0], y[1][0], y[2][0], y[3][0], y[4][0])
        odd = [None] + odd9(y[1][1], y[2][1], y[3][1], y[4][1])
        out[where_q(a, 0)] = even[0]
        for b in range(1, 5):
            out[where_q(a, b)] = even[b] - odd[b]
            out[where_q(a, 9 - b)] = even[b] + odd[b]
    return out


def split(value):
    high = value.astype(jnp.bfloat16)
    return high, (value - high.astype(jnp.float32)).astype(jnp.bfloat16)


def image_blocks(img_ref):
    count = img_ref.shape[0]
    lane = lax.broadcasted_iota(jnp.int32, (count, LANES), 1)
    source = [
        img_ref[:, v * LANES : (v + 1) * LANES].astype(jnp.float32)
        for v in range(img_ref.shape[1] // LANES)
    ]
    per = LANES // STEP
    rows = []
    for p in range(PARTS):
        v, shift = divmod(p * ANG, LANES)
        value = source[v]
        if shift:
            value = jnp.where(
                lane < LANES - shift,
                pltpu.roll(source[v], LANES - shift, 1),
                pltpu.roll(source[v + 1], LANES - shift, 1),
            )
        rows.append(value)
    reach = 1
    while reach < per:
        low = (lane & (reach * STEP)) == 0
        new = list(rows)
        for p in range(per):
            if not p & reach:
                first, second = rows[p], rows[p + reach]
                new[p] = jnp.where(low, first, pltpu.roll(second, reach * STEP, 1))
                new[p + reach] = jnp.where(
                    low, pltpu.roll(first, LANES - reach * STEP, 1), second
                )
        rows = new
        reach *= 2
    for q in range(per, ROT):
        value = None
        for p in range(PARTS):
            v, start = divmod(p * ANG + q * STEP, LANES)
            moved = pltpu.roll(source[v], (p * STEP - start) % LANES, 1)
            if value is None:
                value = moved
            else:
                value = jnp.where(lane < p * STEP, value, moved)
        rows.append(value)
    return rows


def tree(combine, values):
    while len(values) > 1:
        joined = [combine(a, b) for a, b in zip(values[::2], values[1::2])]
        values = joined + values[len(joined) * 2 :]
    return values[0]


def geometry(share):
    piece = min(share, ANG)
    halves = ANG // piece
    pieces = share // piece
    turns = piece // STEP
    width = turns * CLASSES
    padded = -(-(width + CLASSES) // LANES) * LANES
    return piece, halves, pieces, turns, width, padded


def em_kernel(
    count_dev,
    img_hbm,
    refs_hbm,
    sigma_hbm,
    group_hbm,
    bin_hbm,
    ctf_hbm,
    phase_hbm,
    out_ref,
    img_ref,
    refs_ref,
    sigma_ref,
    group_ref,
    bin_ref,
    ctf_ref,
    phase_ref,
    moved,
    fhi,
    flo,
    rhat,
    xs,
    xs_b,
    xp,
    quad_ref,
    sums,
    numh,
    flat,
    cols_t,
    fin,
    mine,
    got,
    pay,
    mid,
    mixed,
    final,
    near_send,
    near_recv,
    far_send,
    far_recv,
    pair_send,
    pair_recv,
    last_send,
    last_recv,
    load_sem,
):
    rows = CLASSES
    count_img = img_ref.shape[0]
    share = refs_ref.shape[1]
    piece, halves, pieces, turns, width, padded = geometry(share)
    group_rows = STEP * pieces
    count_n = fhi.shape[2]
    count_a = 2 * LANES
    half = count_dev // 2
    me = lax.axis_index("img")
    core = lax.rem(me, 2)
    place = lax.div(me, 2)
    partner = me + 1 - 2 * core
    f32, bf16 = jnp.float32, jnp.bfloat16

    def ahead(offset):
        return lax.rem(place + offset, half)

    def behind(offset):
        return lax.rem(place + half - offset, half)

    barrier = pltpu.get_barrier_semaphore()
    for offset in range(1, half):
        pl.semaphore_signal(
            barrier,
            inc=1,
            device_id={"img": 2 * ahead(offset) + core},
            device_id_type=pl.DeviceIdType.MESH,
        )
    pl.semaphore_signal(
        barrier, inc=1, device_id={"img": partner}, device_id_type=pl.DeviceIdType.MESH
    )

    def remote(source, target, send, recv, device):
        return pltpu.make_async_remote_copy(
            src_ref=source,
            dst_ref=target,
            send_sem=send,
            recv_sem=recv,
            device_id={"img": device},
            device_id_type=pl.DeviceIdType.MESH,
        )

    loads = [
        pltpu.make_async_copy(source, target, load_sem.at[index])
        for index, (source, target) in enumerate(
            (
                (refs_hbm, refs_ref),
                (img_hbm, img_ref),
                (sigma_hbm, sigma_ref),
                (group_hbm, group_ref),
                (bin_hbm, bin_ref),
                (ctf_hbm, ctf_ref),
                (phase_hbm, phase_ref),
            )
        )
    ]
    for copy in loads:
        copy.start()
    loads[0].wait()

    fin[...] = refs_ref[...].astype(f32).T
    turned = []
    for q in range(turns):
        turned.append(
            jnp.concatenate(
                [fin[i * piece + q * STEP : i * piece + (q + 1) * STEP, :] for i in range(pieces)],
                axis=0,
            )
        )
    turned.append(jnp.zeros((group_rows, padded - width), f32))
    own = jnp.concatenate(turned, axis=1).astype(bf16)
    mine[...] = own
    got[me] = own
    pl.semaphore_wait(barrier, half)

    far = [
        remote(
            mine,
            got.at[me],
            far_send.at[offset],
            far_recv.at[offset],
            2 * ahead(offset) + core,
        )
        for offset in range(1, half)
    ]
    near = [remote(mine, got.at[me], near_send.at[0], near_recv.at[0], partner)]
    for copy in far + near:
        copy.start()

    for copy in loads[1:]:
        copy.wait()

    blocks = image_blocks(img_ref)

    def pick(ids, table):
        hot = ids == lax.broadcasted_iota(jnp.int32, (table.shape[0], count_img), 0)
        return lax.dot_general(
            hot.astype(f32),
            table,
            (((0,), (0,)), ((), ())),
            precision=EXACT,
            preferred_element_type=f32,
        )

    lane_shell = lax.rem(
        lax.div(lax.broadcasted_iota(jnp.int32, (SHELLS, SPAN), 1), STEP), SHELLS
    )
    spread = (lane_shell == lax.broadcasted_iota(jnp.int32, (SHELLS, SPAN), 0)).astype(f32)
    noise = jnp.dot(
        pick(group_ref[...], sigma_ref[...]), spread, precision=EXACT, preferred_element_type=f32
    )
    ctf = pick(bin_ref[...], ctf_ref[...])
    weight = ctf / noise
    shell_w = jnp.concatenate([ctf * ctf / noise] * (LANES // count_img), axis=0)

    for q in range(ROT):
        at = slice(q * count_img, (q + 1) * count_img)
        value = blocks[q] * weight
        other = pltpu.roll(value, SPAN // 2, 1)
        for slot in (REACH, SIDE):
            moved[slot, 0, at, :] = value
            moved[slot, 1, at, :] = other
        moved[SIDE + 1, 0, at, :] = 0.5 * value
        moved[SIDE + 1, 1, at, :] = 0.5 * value
        for offset in range(1, REACH + 1):
            c = phase_ref[REACH + offset - 1, 0, q : q + 1, :]
            s = phase_ref[REACH + offset - 1, 1, q : q + 1, :]
            vc, os, oc, vs = value * c, other * s, other * c, value * s
            moved[REACH + offset, 0, at, :] = vc + os
            moved[REACH + offset, 1, at, :] = oc - vs
            moved[REACH - offset, 0, at, :] = vc - os
            moved[REACH - offset, 1, at, :] = oc + vs

    both = 2 * count_img

    def feature_tile(tile, carry):
        slot = lax.div(tile, REACH)
        entry = lax.rem(tile, REACH) + REACH * (lax.div(tile, REACH * SIDE)) + REACH * lax.div(
            tile, TILES - 1
        )
        start = pl.multiple_of(tile * both, both)

        def load(q):
            at = slice(q * count_img, (q + 1) * count_img)
            a = moved[slot, 0, at, :] * phase_ref[entry, 0, q : q + 1, :]
            b = moved[slot, 1, at, :] * phase_ref[entry, 1, q : q + 1, :]
            return jnp.concatenate([a + b, a - b], axis=0).astype(bf16).astype(f32)

        for j, pair in enumerate(dft36(load)):
            for part, value in enumerate(pair):
                high, low = split(value)
                fhi[j, part, pl.ds(start, both), :] = high
                flo[j, part, pl.ds(start, both), :] = low
        return carry

    def relay(offset):
        source = 2 * behind(offset) + core
        return remote(
            got.at[source], got.at[source], near_send.at[offset], near_recv.at[offset], partner
        )

    def relay_step(index, carry):
        offset = index + 1
        source = 2 * behind(offset) + core
        remote(
            mine, got.at[source], far_send.at[offset], far_recv.at[offset], partner
        ).wait_recv()
        relay(offset).start()
        first = early + index * per_relay
        lax.fori_loop(first, first + per_relay, feature_tile, 0)
        return carry

    per_relay = 1
    relayed = min(half - 1, TILES // per_relay)
    early = TILES - relayed * per_relay
    lax.fori_loop(0, early, feature_tile, 0)
    lax.fori_loop(0, relayed, relay_step, 0)
    for offset in range(relayed + 1, half):
        far[offset - 1].wait_recv()
        relay(offset).start()
    near += [relay(offset) for offset in range(1, half)]
    for j in range(PAIRS):
        xs_b[j, :, LANES:] = jnp.zeros((2 * rows, LANES), f32)
    for offset in range(half):
        near[offset].wait_recv()

    for h in range(halves):
        for b in range(padded // LANES):
            block = jnp.concatenate(
                [
                    got[g * halves + h][:, b * LANES : (b + 1) * LANES].astype(f32)
                    for g in range(SPAN // group_rows)
                ],
                axis=0,
            )
            flat[h, b * LANES : (b + 1) * LANES, :] = block.T

    def row_of(q):
        return q // turns, (q % turns) * rows

    power = jnp.zeros((rows, SPAN), f32)
    for q in range(ROT):
        h, start = row_of(q)
        block = flat[h, start : start + rows, :]
        power = power + block * block
    unit = 16

    def refs_tile(tile, carry):
        first = pl.multiple_of(tile * unit, unit)

        def load(q):
            h, start = row_of(q)
            return flat[h, pl.ds(start + first, unit), :]

        low_at = 2 * rows
        for j, (re, im) in enumerate(dft36(load)):
            scale = LOG2E / ROT if j == 0 else 2.0 * LOG2E / ROT
            re, im = scale * re, scale * im
            grid = [[re, im], [-im, re]]
            if j == 0:
                zero = jnp.zeros_like(re)
                grid = [[re, zero], [zero, im]]
            for r in range(2):
                for c in range(2):
                    high, low = split(grid[r][c])
                    rhat[j, c, pl.ds(first + r * rows, unit), :] = high
                    rhat[j, c, pl.ds(first + r * rows + low_at, unit), :] = low
        return carry

    lax.fori_loop(0, rows // unit, refs_tile, 0)
    quad_ref[...] = (0.5 * LOG2E) * lax.dot_general(
        power, shell_w, (((1,), (1,)), ((), ())), precision=EXACT, preferred_element_type=f32
    )

    def both_halves(ref, j):
        return jnp.concatenate([ref[j, 0], ref[j, 1]], axis=1)

    for j in range(PAIRS):
        left = both_halves(rhat, j)
        wide = lax.dot_general(
            left, both_halves(fhi, j), (((1,), (1,)), ((), ())), preferred_element_type=f32
        )
        rest = lax.dot_general(
            left[: 2 * rows],
            both_halves(flo, j),
            (((1,), (1,)), ((), ())),
            preferred_element_type=f32,
        )
        value = wide[: 2 * rows] + wide[2 * rows :] + rest
        xs[j] = value[:, :count_a]
        xs_b[j, :, : count_n - count_a] = value[:, count_a:]

    row_tiles = rows // 8
    lane = lax.broadcasted_iota(jnp.int32, (8, LANES), 1)
    packed_lanes = row_tiles * count_img
    spots = [(r // 2, r % 2) for r in range(ROT)]

    def load_unit(ref, k, t, j, part):
        return ref[j, pl.ds(k + part * rows, 8), t * LANES : (t + 1) * LANES]

    def score_unit(pairs, put, best):
        values = idft36(pairs)
        for r, value in enumerate(values):
            put(*spots[r], value)
        return jnp.maximum(best, tree(jnp.maximum, values))

    def put_unit(ref, k, t):
        def put(j, part, value):
            ref[j, pl.ds(k + part * rows, 8), t * LANES : (t + 1) * LANES] = value

        return put

    def score_units(units, best):
        loaded = []
        for ref, k, t in units:
            pairs = [
                tuple(load_unit(ref, k, t, j, part) for part in range(2)) for j in range(PAIRS)
            ]
            pairs[0] = (pairs[0][0] - quad_ref[pl.ds(k, 8), :], pairs[0][1])
            loaded.append(pairs)
        solved = [idft36(pairs) for pairs in loaded]
        for unit, values in zip(units, solved):
            for r, value in enumerate(values):
                put_unit(*unit)(*spots[r], value)
        return tuple(
            jnp.maximum(old, tree(jnp.maximum, values)) for old, values in zip(best, solved)
        )

    def score_pair(index, best):
        k = pl.multiple_of(index * 8, 8)
        return score_units([(xs, k, 0), (xs, k, 1)], best)

    def score_pair_b(index, best):
        k = pl.multiple_of(index * 16, 16)
        return score_units([(xs_b, k, 0), (xs_b, k + 8, 0)], best)

    best = jnp.full((8, LANES), -BIG, f32)
    best = lax.fori_loop(0, row_tiles, score_pair, (best, best))
    best = lax.fori_loop(0, row_tiles // 2, score_pair_b, best)
    best = jnp.maximum(*best)

    def side_by_side(load):
        value = load(0)
        for k in range(1, row_tiles):
            value = jnp.where(
                lane < k * count_img, value, pltpu.roll(load(k), k * count_img, 1)
            )
        return value

    pairs = [
        tuple(side_by_side(lambda k: load_unit(xs_b, k * 8, 1, j, part)) for part in range(2))
        for j in range(PAIRS)
    ]
    shared = side_by_side(lambda k: quad_ref[k * 8 : (k + 1) * 8, :])
    pairs[0] = (jnp.where(lane < packed_lanes, pairs[0][0] - shared, -BIG), pairs[0][1])

    def put_packed(j, part, value):
        xp[j, part * 8 : (part + 1) * 8, :] = value

    best = score_unit(pairs, put_packed, best)

    def fold(value, combine):
        reach = count_img
        while reach < LANES:
            value = combine(value, pltpu.roll(value, reach, 1))
            reach *= 2
        return jnp.concatenate([value] * 8, axis=0)

    top = fold(jnp.max(best, axis=0, keepdims=True), jnp.maximum)
    sums[0] = top

    def exp_unit(get, put):
        high = sums[0]
        scores = [get(*spot) for spot in spots]
        pairs = dft36(lambda q: jnp.exp2(scores[q] - high))
        for j, pair in enumerate(pairs):
            for part, value in enumerate(pair):
                put(j, part, value)
        return pairs[0][0]

    def exp_tile(ref, k, t):
        def put(j, part, value):
            ref[j, pl.ds(k + part * rows, 8), t * LANES : (t + 1) * LANES] = value

        return exp_unit(lambda j, part: load_unit(ref, k, t, j, part), put)

    def exp_pair(index, total):
        k = pl.multiple_of(index * 8, 8)
        return total + exp_tile(xs, k, 0) + exp_tile(xs, k, 1)

    def exp_pair_b(index, total):
        k = pl.multiple_of(index * 16, 16)
        return total + exp_tile(xs_b, k, 0) + exp_tile(xs_b, k + 8, 0)

    total = exp_unit(lambda j, part: xp[j, part * 8 : (part + 1) * 8, :], put_packed)
    total = lax.fori_loop(0, row_tiles, exp_pair, total)
    total = lax.fori_loop(0, row_tiles // 2, exp_pair_b, total)
    norm = fold(jnp.sum(total, axis=0, keepdims=True), jnp.add)
    scale = 1.0 / norm
    scale_row = jnp.concatenate([scale[:1]] * 4, axis=1)
    for j in range(PAIRS):
        for part in range(2):
            value = xp[j, part * 8 : (part + 1) * 8, :]
            for k in range(row_tiles):
                at = slice(part * rows + k * 8, part * rows + (k + 1) * 8)
                xs_b[j, at, LANES:] = (
                    pltpu.roll(value, LANES - k * count_img, 1) if k else value
                )

    occupancy = []
    for k in range(row_tiles):
        at = slice(k * 8, (k + 1) * 8)
        rest = jnp.where(lane < count_img, xs_b[0, at, LANES:], 0.0)
        occupancy.append(
            (xs[0, at, :LANES] + xs[0, at, LANES:] + xs_b[0, at, :LANES] + rest) * scale
        )
    field = jnp.dot(
        jnp.concatenate(occupancy, axis=0), shell_w, precision=EXACT, preferred_element_type=f32
    )
    high = field.astype(bf16).astype(f32)
    first_lane = lax.rem(lax.broadcasted_iota(jnp.int32, (rows, SPAN), 1), STEP) == 0
    field = jnp.where(first_lane, high, field - high)

    for j in range(PAIRS):
        left = jnp.concatenate([xs[j], xs_b[j]], axis=1)
        left = (left * scale_row).astype(bf16)[:, :count_n]
        value = jnp.dot(left, both_halves(fhi, j), preferred_element_type=f32)
        if j:
            numh[j, :rows] = value[:rows, :SPAN] + value[rows:, SPAN:]
            numh[j, rows:] = value[:rows, SPAN:] - value[rows:, :SPAN]
        else:
            numh[j, :rows] = 0.5 * value[:rows, :SPAN]
            numh[j, rows:] = 0.5 * value[rows:, SPAN:]

    def number_tile(tile, carry):
        k = pl.multiple_of(tile * 8, 8)
        pairs = [
            tuple(numh[j, pl.ds(k + part * rows, 8), :] for part in range(2)) for j in range(PAIRS)
        ]
        for q, value in enumerate(idft36(pairs)):
            h, start = row_of(q)
            flat[h, pl.ds(start + k, 8), :] = value
        return carry

    lax.fori_loop(0, row_tiles, number_tile, 0)
    for h in range(halves):
        flat[h, width : width + rows, :] = field
        if padded > width + rows:
            flat[h, width + rows :, :] = jnp.zeros((padded - width - rows, SPAN), f32)
        for b in range(padded // LANES):
            block = flat[h, b * LANES : (b + 1) * LANES, :].T
            for g in range(SPAN // group_rows):
                cols_t[h, g, :, b * LANES : (b + 1) * LANES] = block[
                    g * group_rows : (g + 1) * group_rows
                ]

    def block_for(device):
        return cols_t[lax.rem(device, halves), lax.div(device, halves)]

    pairs = []
    for offset in [*range(1, half), 0]:
        slot = ahead(offset)
        pay[offset] = block_for(2 * slot + 1 - core).astype(bf16)
        copy = remote(
            pay.at[offset], mid.at[offset], pair_send.at[offset], pair_recv.at[offset], partner
        )
        copy.start()
        pairs.append(copy)

    lasts = []
    for index, offset in enumerate([*range(1, half), 0]):
        own = block_for(2 * ahead(offset) + core)
        pairs[index].wait_recv()
        value = own + mid[offset].astype(f32)
        if offset:
            mixed[offset] = value.astype(bf16)
            copy = remote(
                mixed.at[offset],
                final.at[offset],
                last_send.at[offset],
                last_recv.at[offset],
                2 * ahead(offset) + core,
            )
            copy.start()
            lasts.append(copy)
        else:
            result = value
    for index, copy in enumerate(lasts):
        copy.wait_recv()
        result = result + final[index + 1].astype(f32)
    weights = result[:, width : width + rows]
    for i in range(pieces):
        inverse = weights[i * STEP : i * STEP + 1] + weights[i * STEP + 1 : i * STEP + 2] + 1.0
        inverse = (2.0 / ROT) / inverse
        for q in range(turns):
            fin[i * piece + q * STEP : i * piece + (q + 1) * STEP, :] = (
                result[i * STEP : (i + 1) * STEP, q * rows : (q + 1) * rows] * inverse
            )
    out_ref[...] = fin[...].T
    for copy in far + near + pairs + lasts:
        copy.wait_send()


def on_device(images, class_refs, sigma2, ctf_group, defocus_bin):
    count_dev = lax.axis_size("img")
    half = count_dev // 2
    count_img = images.shape[0]
    share = class_refs.shape[1]
    piece, halves, pieces, turns, width, padded = geometry(share)
    group_rows = STEP * pieces
    count_n = (SHIFTS + 1) * count_img
    travel = pltpu.VMEM((half, group_rows, padded), jnp.bfloat16)
    args = (
        images,
        class_refs,
        sigma2,
        ctf_group.reshape(1, count_img),
        defocus_bin.reshape(1, count_img),
        jnp.asarray(ctf_lanes()),
        jnp.asarray(phase_parts()),
    )
    return pl.pallas_call(
        lambda *refs: em_kernel(count_dev, *refs),
        out_shape=jax.ShapeDtypeStruct(class_refs.shape, jnp.float32),
        in_specs=[pl.BlockSpec(memory_space=pl.ANY)] * 7,
        out_specs=pl.BlockSpec(memory_space=pltpu.VMEM),
        scratch_shapes=[pltpu.VMEM(arg.shape, arg.dtype) for arg in args]
        + [
            pltpu.VMEM((SLOTS, 2, ROT * count_img, SPAN), jnp.float32),
            pltpu.VMEM((PAIRS, 2, count_n, SPAN), jnp.bfloat16),
            pltpu.VMEM((PAIRS, 2, count_n, SPAN), jnp.bfloat16),
            pltpu.VMEM((PAIRS, 2, 4 * CLASSES, SPAN), jnp.bfloat16),
            pltpu.VMEM((PAIRS, 2 * CLASSES, 2 * LANES), jnp.float32),
            pltpu.VMEM((PAIRS, 2 * CLASSES, 2 * LANES), jnp.float32),
            pltpu.VMEM((PAIRS, 16, LANES), jnp.float32),
            pltpu.VMEM((CLASSES, LANES), jnp.float32),
            pltpu.VMEM((1, 8, LANES), jnp.float32),
            pltpu.VMEM((PAIRS, 2 * CLASSES, SPAN), jnp.float32),
            pltpu.VMEM((halves, padded, SPAN), jnp.float32),
            pltpu.VMEM((halves, SPAN // group_rows, group_rows, padded), jnp.float32),
            pltpu.VMEM((share, CLASSES), jnp.float32),
            pltpu.VMEM((group_rows, padded), jnp.bfloat16),
            pltpu.VMEM((count_dev, group_rows, padded), jnp.bfloat16),
            travel,
            travel,
            travel,
            travel,
        ]
        + [pltpu.SemaphoreType.DMA((half,))] * 8
        + [pltpu.SemaphoreType.DMA((len(args),))],
        compiler_params=pltpu.CompilerParams(
            vmem_limit_bytes=60 * 2**20, collective_id=0, has_side_effects=True
        ),
        name="em_step",
    )(*args)


def solution(mesh):
    in_specs = (
        P(("groups", "img"), None),
        P("groups", "img"),
        P("groups", None),
        P(("groups", "img")),
        P(("groups", "img")),
    )
    out_specs = P("groups", "img")
    return jax.shard_map(
        on_device, mesh=mesh, in_specs=in_specs, out_specs=out_specs, check_vma=False
    )
```
